32 devices in a mesh: row: 8 (over y, x, core), col: 4 (over z).
Axes of the slice: x: 2, y: 2, z: 4, core: 2. Of those that a mesh axis runs over, the one named last changes fastest.
Arguments:
- alignment: float32 [32, 384, 64], P('col', 'row'), may hold values from -6 to 6
- pair_rep: float32 [384, 384, 128], P('row', 'col'), may hold values from -6 to 6
- seq_mask: int32 [32], P('col'), may hold values 0 or 1
- res_mask: int32 [384], P('row'), may hold values 0 or 1
- left_weight: float32 [64, 32], replicated, may hold values from -0.75 to 0.75
- right_weight: float32 [64, 32], replicated, may hold values from -0.75 to 0.75
- w_outer: float32 [1024, 128], replicated, may hold values from -4 to 4
- w_logits: float32 [128, 8], replicated, may hold values from -45 to 45
- value_weight: float32 [64, 256], replicated, may hold values from -0.75 to 0.75
- gate_weight: float32 [64, 256], replicated, may hold values from -0.75 to 0.75
- output_weight: float32 [256, 64], replicated, may hold values from -6 to 6
Outputs:
- alignment_out: float32 [32, 384, 64], P('col', 'row')
- pair_out: float32 [384, 384, 128], P('row', 'col')
The draws below stay inside these ranges and needn't reach their ends.
All inputs are finite; a program needn't handle non-finite values. No bound on the sum of `seq_mask` or of `res_mask` on one device may be relied on, other than what follows from the above.
Results may differ from the reference program's by a relative error of at most 0.0003.
Values sent between devices are 32-bit elements; how exact they have to be, the bound alone decides.
A program may use at most 128 MiB of HBM per device.

```python
import jax
import jax.numpy as jnp
from jax import lax

ALIGNED_WIDTH = 64
FACTOR_WIDTH = 32
PAIR_W = 128
AVERAGE_HEADS = 8
HEAD_CHANNELS = 32
RES_DEV = 48
SEQUENCE_COUNT = 32
RESIDUE_COUNT = 384
OUTER = 1024
N_ROW = 8


def draw_w_logits(key, part):
    first_key, second_key = jax.random.split(jax.random.fold_in(key, 11))
    normal_part = jnp.clip(jax.random.normal(first_key, (PAIR_W, AVERAGE_HEADS), jnp.float32), -5.0, 5.0)
    base = normal_part / PAIR_W ** 0.5
    levels = jnp.exp(jnp.linspace(jnp.log(0.5), jnp.log(2.0), AVERAGE_HEADS))
    shuffled = jax.random.permutation(second_key, AVERAGE_HEADS)
    return base * levels[shuffled][None, :]


def plant(array, key, smallest, top_value):
    extent = array.shape
    index_at = [jax.random.randint(jax.random.fold_in(key, axis), (), 0, extent[axis]) for axis in range(len(extent))]
    array = array.at[tuple(index_at)].set(smallest)
    longest = extent.index(max(extent))
    index_at[longest] = (index_at[longest] + 1) % extent[longest]
    return array.at[tuple(index_at)].set(top_value)


def level_of(stream_key, shape, cuts, low, largest):
    level = 1.0
    for position, parts in cuts:
        steps = jax.random.uniform(jax.random.fold_in(jax.random.fold_in(stream_key, 6), position), (parts,), jnp.float32, low / len(cuts), largest / len(cuts))
        level = level * jnp.repeat(jnp.exp(steps), shape[position] // parts).reshape((-1,) + (1,) * (len(shape) - 1 - position))
    return level


def gaussian(rng, dims, width, bound, pieces=(), dtype=jnp.bfloat16):
    result = width * jax.random.normal(rng, dims, jnp.float32)
    if pieces:
        result = result * level_of(rng, dims, pieces, -0.22, 0.18)
    return jnp.clip(result, -bound, bound).astype(dtype)


def setup_inputs(seed: int = 0) -> dict:
    arg_keys = jax.random.split(jax.random.key(seed), 12)
    alignment = gaussian(arg_keys[0], (SEQUENCE_COUNT, RESIDUE_COUNT, ALIGNED_WIDTH), 1.0, 6.0, ((0, 4), (1, 8)), jnp.float32)
    pair_rep = gaussian(arg_keys[1], (RESIDUE_COUNT, RESIDUE_COUNT, PAIR_W), 1.0, 6.0, ((0, 8), (1, 4)), jnp.float32)
    seq_mask = plant((jax.random.randint(arg_keys[2], (SEQUENCE_COUNT,), 0, 8) < 7).astype(jnp.int32), jax.random.fold_in(arg_keys[2], 1), 0, 1)
    res_mask = plant((jax.random.randint(arg_keys[3], (RESIDUE_COUNT,), 0, 8) < 7).astype(jnp.int32), jax.random.fold_in(arg_keys[3], 1), 0, 1)
    left_weight = gaussian(arg_keys[4], (ALIGNED_WIDTH, FACTOR_WIDTH), ALIGNED_WIDTH ** -0.5, 0.75, (), jnp.float32)
    right_weight = gaussian(arg_keys[5], (ALIGNED_WIDTH, FACTOR_WIDTH), ALIGNED_WIDTH ** -0.5, 0.75, (), jnp.float32)
    w_outer = gaussian(arg_keys[6], (OUTER, PAIR_W), 0.3, 4.0, (), jnp.float32)
    w_logits = draw_w_logits(jax.random.fold_in(arg_keys[11], 71), 0)
    value_weight = gaussian(arg_keys[8], (ALIGNED_WIDTH, AVERAGE_HEADS * HEAD_CHANNELS), ALIGNED_WIDTH ** -0.5, 0.75, (), jnp.float32)
    gate_weight = gaussian(arg_keys[9], (ALIGNED_WIDTH, AVERAGE_HEADS * HEAD_CHANNELS), ALIGNED_WIDTH ** -0.5, 0.75, (), jnp.float32)
    output_weight = gaussian(arg_keys[10], (AVERAGE_HEADS * HEAD_CHANNELS, ALIGNED_WIDTH), 0.5, 6.0, (), jnp.float32)
    return {"alignment": alignment, "pair_rep": pair_rep, "seq_mask": seq_mask, "res_mask": res_mask, "left_weight": left_weight, "right_weight": right_weight, "w_outer": w_outer, "w_logits": w_logits, "value_weight": value_weight, "gate_weight": gate_weight, "output_weight": output_weight}


epsilon = 1e-05
highest = lax.Precision.HIGHEST

def layer_norm(values):
    center = lax.optimization_barrier(jnp.mean(values, axis=-1, keepdims=True))
    centred = values - center
    return centred * lax.rsqrt(lax.optimization_barrier(jnp.mean(centred * centred, axis=-1, keepdims=True)) + epsilon)

def project(values, weight):
    return jnp.einsum('...c,cv->...v', values, weight, precision=highest)

def outer_block(left_rows, right_rows, w_outer):
    outer = jnp.einsum('sia,sjb->ijab', left_rows, right_rows, precision=highest)
    flat = outer.reshape(outer.shape[0] * outer.shape[1], outer.shape[2] * outer.shape[3])
    mapped = jnp.dot(flat, w_outer, precision=highest, preferred_element_type=jnp.float32)
    return mapped.reshape(outer.shape[0], outer.shape[1], w_outer.shape[1])

def reference(alignment, pair_rep, seq_mask, res_mask, left_weight, right_weight, w_outer, w_logits, value_weight, gate_weight, output_weight):
    normed = layer_norm(alignment)
    seq_live = seq_mask.astype(jnp.float32)
    res_live = res_mask.astype(jnp.float32)
    live = (seq_live[:, None] * res_live[None, :])[:, :, None]
    left_proj = project(normed, left_weight) * live
    right_proj = project(normed, right_weight) * live
    left_blocks = left_proj.reshape(SEQUENCE_COUNT, N_ROW, RES_DEV, FACTOR_WIDTH).transpose(1, 0, 2, 3)
    outer_sums = lax.map(lambda row_block: outer_block(row_block, right_proj, w_outer), left_blocks)
    outer_sums = outer_sums.reshape(RESIDUE_COUNT, RESIDUE_COUNT, PAIR_W)
    pair_count = jnp.maximum(res_live[:, None] * res_live[None, :] * jnp.sum(seq_live), 1.0)
    pair_out = pair_rep + outer_sums / pair_count[:, :, None]
    pair_normed = layer_norm(pair_out)
    logits = jnp.einsum('ijz,zh->hij', pair_normed, w_logits, precision=highest)
    logits = logits + ((res_live - 1.0) * 1000000000.0)[None, None, :]
    row_max = lax.optimization_barrier(jnp.max(logits, axis=2, keepdims=True))
    expo_terms = jnp.exp(logits - row_max)
    weights = expo_terms / lax.optimization_barrier(jnp.sum(expo_terms, axis=2, keepdims=True))
    values = project(normed, value_weight).reshape(SEQUENCE_COUNT, RESIDUE_COUNT, AVERAGE_HEADS, HEAD_CHANNELS)
    averaged = jnp.einsum('hij,sjhv->sihv', weights, values, precision=highest)
    averaged = averaged.reshape(SEQUENCE_COUNT, RESIDUE_COUNT, AVERAGE_HEADS * HEAD_CHANNELS)
    gate_open = jax.nn.sigmoid(project(normed, gate_weight))
    alignment_out = alignment + project(gate_open * averaged, output_weight)
    return (alignment_out, pair_out)
```

```python
import functools

import jax
import jax.numpy as jnp
from jax import lax
from jax.experimental import pallas as pl
from jax.experimental.pallas import tpu as pltpu
from jax.sharding import PartitionSpec as P

MESH = pl.DeviceIdType.MESH
F32 = jnp.float32
BF16 = jnp.bfloat16
epsilon = 1e-05
VMEM_LIMIT = 60 * 1024 * 1024


def layer_norm(values):
    center = jnp.mean(values, axis=-1, keepdims=True)
    centred = values - center
    return centred * lax.rsqrt(jnp.mean(centred * centred, axis=-1, keepdims=True) + epsilon)


def split(values):
    high = values.astype(BF16)
    return high, (values - high.astype(F32)).astype(BF16)


def dot(left, right):
    return jnp.dot(left, right, preferred_element_type=F32)


def dot_split(left, right_high, right_low):
    high, low = split(left)
    return dot(high, right_high) + (dot(low, right_high) + dot(high, right_low))


def exchange_kernel(
    n_row,
    n_col,
    ratio,
    seq_ref,
    res_ref,
    align_ref,
    left_w_ref,
    right_w_ref,
    left_out,
    right_out,
    norm_out,
    rows_buf,
    masked_buf,
    block_buf,
    left_buf,
    right_buf,
    norm_buf,
    left_send,
    left_recv,
    right_send,
    right_recv,
    norm_send,
    norm_recv,
):
    row, col = lax.axis_index("row"), lax.axis_index("col")
    n = n_row * n_col
    me = row * n_col + col
    barrier = pltpu.get_barrier_semaphore()

    def greet(step, carry):
        other = lax.rem(me + step, n)
        pl.semaphore_signal(
            barrier,
            inc=1,
            device_id=(other // n_col, lax.rem(other, n_col)),
            device_id_type=MESH,
        )
        return carry

    lax.fori_loop(1, n, greet, 0)
    seqs, rows, width = align_ref.shape
    res_row = res_ref[...].astype(F32)
    diag = lax.broadcasted_iota(jnp.int32, (rows, rows), 0) == lax.broadcasted_iota(
        jnp.int32, (rows, rows), 1
    )
    res_col = jnp.sum(
        jnp.where(diag, jnp.broadcast_to(res_row, (rows, rows)), 0.0), axis=1, keepdims=True
    )
    lane_seq = lax.rem(lax.broadcasted_iota(jnp.int32, (width, right_w_ref.shape[1]), 1), seqs)
    seq_sum = 0.0
    for s in range(seqs):
        normed = layer_norm(align_ref[s])
        norm_buf[:, s * width : (s + 1) * width] = normed
        live = seq_ref[s].astype(F32)
        seq_sum = seq_sum + live
        masked = normed * (res_col * live)
        masked_buf[:, s * width : (s + 1) * width] = masked
        rows_buf[pl.ds(s, rows, stride=seqs), :] = masked
        block_buf[s * width : (s + 1) * width, :] = jnp.where(lane_seq == s, right_w_ref[...], 0.0)
    wl_high, wl_low = split(left_w_ref[...])
    left = dot_split(rows_buf[...], wl_high, wl_low)
    quarter = left.shape[0] // 4
    factor = left.shape[1]
    for g in range(4):
        left_buf[0:quarter, g * factor : (g + 1) * factor] = left[g * quarter : (g + 1) * quarter]
    left_buf[quarter : quarter + 8, :] = jnp.full((8, left_buf.shape[1]), seq_sum, F32)
    wr_high, wr_low = split(block_buf[...])
    right_buf[0:rows, :] = dot_split(masked_buf[...], wr_high, wr_low)
    right_buf[rows : rows + 8, 0:rows] = jnp.broadcast_to(res_row, (8, rows))
    right_buf[rows : rows + 8, rows:] = jnp.zeros((8, right_buf.shape[1] - rows), F32)

    pl.semaphore_wait(barrier, n - 1)
    dest = row // ratio
    spot = lax.rem(row, ratio)
    started = []
    for k in range(1, n_col):
        peer = lax.rem(col + k, n_col)
        copy = pltpu.make_async_remote_copy(
            left_buf,
            left_out.at[col],
            left_send.at[k],
            left_recv.at[n_col - k],
            device_id=(row, peer),
            device_id_type=MESH,
        )
        copy.start()
        started.append(copy)
    away = dest != col
    for k in range(1, n_row):
        copy = pltpu.make_async_remote_copy(
            right_buf,
            right_out.at[spot, col],
            right_send.at[k],
            right_recv.at[spot, col],
            device_id=(lax.rem(row + k, n_row), dest),
            device_id_type=MESH,
        )
        copy.start()
    own_remote = pltpu.make_async_remote_copy(
        right_buf,
        right_out.at[spot, col],
        right_send.at[0],
        right_recv.at[spot, col],
        device_id=(row, dest),
        device_id_type=MESH,
    )
    own_local = pltpu.make_async_copy(right_buf, right_out.at[spot, col], right_recv.at[spot, col])

    @pl.when(away)
    def _():
        own_remote.start()

    @pl.when(jnp.logical_not(away))
    def _():
        own_local.start()

    for k in range(1, n_row):
        peer = lax.rem(row + k, n_row)
        copy = pltpu.make_async_remote_copy(
            norm_buf,
            norm_out.at[row],
            norm_send.at[k],
            norm_recv.at[n_row - k],
            device_id=(peer, col),
            device_id_type=MESH,
        )
        copy.start()
        started.append(copy)
    left_own = pltpu.make_async_copy(left_buf, left_out.at[col], left_recv.at[0])
    left_own.start()
    norm_own = pltpu.make_async_copy(norm_buf, norm_out.at[row], norm_recv.at[0])
    norm_own.start()
    left_own.wait()
    norm_own.wait()
    for copy in started:
        copy.wait_send()
    for k in range(1, n_row):
        pltpu.make_async_copy(right_buf, right_buf, right_send.at[k]).wait()

    @pl.when(away)
    def _():
        own_remote.wait_send()

    for k in range(1, n_col):
        src = lax.rem(col + k, n_col)
        pltpu.make_async_copy(left_buf, left_out.at[src], left_recv.at[k]).wait()
    for t in range(ratio):
        for c in range(n_col):
            pltpu.make_async_copy(right_buf, right_out.at[t, c], right_recv.at[t, c]).wait()
    for k in range(1, n_row):
        src = lax.rem(row + k, n_row)
        pltpu.make_async_copy(norm_buf, norm_out.at[src], norm_recv.at[k]).wait()


def pair_kernel(
    left_ref,
    right_ref,
    outer_ref,
    logits_w_ref,
    pair_ref,
    pair_out,
    logits_out,
    w_buf,
    l_buf,
    r_buf,
    mask_buf,
    high_buf,
    low_buf,
):
    n_col = left_ref.shape[0]
    quarter = left_ref.shape[1] - 8
    ratio, rows = right_ref.shape[0], right_ref.shape[2] - 8
    k_col = right_ref.shape[3]
    factor = w_buf.shape[0] // 3
    here, cols, width = pair_ref.shape
    heads = logits_w_ref.shape[0] // 2
    seqs = k_col // factor
    step = pl.program_id(0)

    @pl.when(step == 0)
    def _():
        for b in range(factor):
            high, low = split(outer_ref[pl.ds(b, factor, stride=factor), :])
            lanes = slice(b * width, (b + 1) * width)
            w_buf[0:factor, lanes] = high
            w_buf[factor : 2 * factor, lanes] = low
            w_buf[2 * factor : 3 * factor, lanes] = high
        count = left_ref[0, quarter : quarter + 1, 0:1]
        for c in range(1, n_col):
            count = count + left_ref[c, quarter : quarter + 1, 0:1]
        scale = 1.0 / jnp.maximum(count, 1.0)
        for c in range(n_col):
            packed = left_ref[c, 0:quarter, :] * scale
            high = packed.astype(BF16).astype(F32)
            low = packed - high
            for g in range(4):
                lanes = slice(g * factor, (g + 1) * factor)
                parts = [high[:, lanes], high[:, lanes], low[:, lanes]]
                l_buf[c, g * quarter : (g + 1) * quarter, :] = jnp.concatenate(
                    parts, axis=1
                ).astype(BF16)
            for t in range(ratio):
                high_r, low_r = split(right_ref[t, c, 0:rows, :])
                lanes = slice(c * k_col, (c + 1) * k_col)
                r_buf[t * rows : (t + 1) * rows, lanes] = high_r
                r_buf[cols + t * rows : cols + (t + 1) * rows, lanes] = low_r
        for t in range(ratio):
            mask_buf[:, t * rows : (t + 1) * rows] = (
                right_ref[t, 0, rows : rows + 8, 0:rows] - 1.0
            ) * 1000000000.0

    group = here * seqs
    l_rows = jnp.concatenate(
        [l_buf[c, pl.ds(pl.multiple_of(step * group, group), group), :] for c in range(n_col)],
        axis=0,
    )
    for nb in range(factor // 2):
        mixed = dot(l_rows, w_buf[:, nb * 2 * width : (nb + 1) * 2 * width])
        tiles = jnp.concatenate(
            [
                mixed[:, :width].reshape(n_col * here, seqs, width),
                mixed[:, width:].reshape(n_col * here, seqs, width),
            ],
            axis=1,
        )
        high, low = split(tiles)
        for c in range(n_col):
            high_buf[:, c, nb] = high[c * here : (c + 1) * here]
            low_buf[:, c, nb] = low[c * here : (c + 1) * here]
    depth = n_col * k_col
    r_both = r_buf[...]
    w_both = logits_w_ref[...]
    nt = (((1,), (1,)), ((), ()))
    for p in range(here // 2):
        right_high = jnp.concatenate(
            [high_buf[2 * p + t].reshape(depth, width) for t in range(2)], axis=1
        )
        right_low = jnp.concatenate(
            [low_buf[2 * p + t].reshape(depth, width) for t in range(2)], axis=1
        )
        first = dot(r_both, right_high)
        sums = first[:cols] + (first[cols:] + dot(r_both[:cols], right_low))
        for t in range(2):
            i = 2 * p + t
            pair = pair_ref[i] + sums[:, t * width : (t + 1) * width]
            pair_out[i] = pair
            high, low = split(layer_norm(pair))
            one = lax.dot_general(w_both, high, nt, preferred_element_type=F32)
            two = lax.dot_general(w_both, low, nt, preferred_element_type=F32)
            logits = one[:heads] + (one[heads:] + two[:heads])
            logits_out[i * heads : (i + 1) * heads, :] = logits + mask_buf[...]


def average_kernel(
    n_col,
    logits_ref,
    norm_ref,
    align_ref,
    value_w_ref,
    gate_w_ref,
    output_w_ref,
    out_ref,
    slots,
    sends,
    recvs,
):
    row, col = lax.axis_index("row"), lax.axis_index("col")
    barrier = pltpu.get_barrier_semaphore()
    for k in range(1, n_col):
        pl.semaphore_signal(
            barrier, inc=1, device_id=(row, lax.rem(col + k, n_col)), device_id_type=MESH
        )
    pl.semaphore_wait(barrier, n_col - 1)
    copies = []
    for k in range(1, n_col):
        copy = pltpu.make_async_remote_copy(
            logits_ref,
            slots.at[col],
            sends.at[k],
            recvs.at[n_col - k],
            device_id=(row, lax.rem(col + k, n_col)),
            device_id_type=MESH,
        )
        copy.start()
        copies.append(copy)
    own = pltpu.make_async_copy(logits_ref, slots.at[col], recvs.at[0])
    own.start()
    seqs, rows, width = align_ref.shape
    total_rows, cols = logits_ref.shape
    heads = total_rows // rows
    channels = value_w_ref.shape[1]
    head_width = channels // heads
    wv_high, wv_low = split(value_w_ref[...])
    wg_high, wg_low = split(gate_w_ref[...])
    wo_high, wo_low = split(output_w_ref[...])
    own_head = (
        lax.broadcasted_iota(jnp.int32, (heads, channels), 1) // head_width
        == lax.broadcasted_iota(jnp.int32, (heads, channels), 0)
    ).astype(F32)
    own.wait()
    for copy in copies:
        copy.wait_send()
    for k in range(1, n_col):
        src = lax.rem(col + k, n_col)
        pltpu.make_async_copy(logits_ref, slots.at[src], recvs.at[k]).wait()
    top = jnp.max(slots[0], axis=1, keepdims=True)
    for c in range(1, n_col):
        top = jnp.maximum(top, jnp.max(slots[c], axis=1, keepdims=True))
    total = jnp.zeros_like(top)
    for c in range(n_col):
        terms = jnp.exp(slots[c] - top)
        slots[c] = terms
        total = total + jnp.sum(terms, axis=1, keepdims=True)
    inverse = 1.0 / total
    mixed = None
    for c in range(n_col):
        high, low = split(norm_ref[c * cols : (c + 1) * cols, :])
        part = dot_split(slots[c] * inverse, high, low)
        mixed = part if mixed is None else mixed + part
    for s in range(seqs):
        wide = dot_split(mixed[:, s * width : (s + 1) * width], wv_high, wv_low)
        averaged = jnp.sum(wide.reshape(rows, heads, channels) * own_head[None], axis=1)
        align = align_ref[s]
        gate = jax.nn.sigmoid(dot_split(layer_norm(align), wg_high, wg_low))
        out_ref[s] = align + dot_split(gate * averaged, wo_high, wo_low)


def per_device(
    n_row,
    n_col,
    alignment,
    pair_rep,
    seq_mask,
    res_mask,
    left_weight,
    right_weight,
    w_outer,
    w_logits,
    value_weight,
    gate_weight,
    output_weight,
):
    seqs, rows, width = alignment.shape
    cols, pair_width = pair_rep.shape[1], pair_rep.shape[2]
    factor = left_weight.shape[1]
    heads = w_logits.shape[1]
    ratio = cols // rows
    k_col = factor * seqs
    quarter = rows * seqs // 4
    vmem = pl.BlockSpec(memory_space=pltpu.VMEM)
    smem = pl.BlockSpec(memory_space=pltpu.SMEM)
    dma = pltpu.SemaphoreType.DMA
    left_shape = (quarter + 8, 4 * factor)
    right_shape = (rows + 8, k_col)
    norm_shape = (rows, seqs * width)
    left_all, right_all, norm_all = pl.pallas_call(
        functools.partial(exchange_kernel, n_row, n_col, ratio),
        out_shape=(
            jax.ShapeDtypeStruct((n_col,) + left_shape, F32),
            jax.ShapeDtypeStruct((ratio, n_col) + right_shape, F32),
            jax.ShapeDtypeStruct((n_row,) + norm_shape, F32),
        ),
        in_specs=[smem, vmem, vmem, vmem, vmem],
        out_specs=(vmem, vmem, vmem),
        scratch_shapes=[
            pltpu.VMEM((rows * seqs, width), F32),
            pltpu.VMEM(norm_shape, F32),
            pltpu.VMEM((seqs * width, k_col), F32),
            pltpu.VMEM(left_shape, F32),
            pltpu.VMEM(right_shape, F32),
            pltpu.VMEM(norm_shape, F32),
            dma((n_col,)),
            dma((n_col,)),
            dma((n_row,)),
            dma((ratio, n_col)),
            dma((n_row,)),
            dma((n_row,)),
        ],
        compiler_params=pltpu.CompilerParams(
            collective_id=0, has_side_effects=True, vmem_limit_bytes=VMEM_LIMIT
        ),
        name="exchange",
    )(
        seq_mask,
        res_mask.reshape(1, rows),
        alignment,
        left_weight,
        jnp.repeat(right_weight, seqs, axis=1),
    )
    here = 8
    wt = w_logits.T
    wt_high = wt.astype(BF16)
    wt_low = (wt - lax.reduce_precision(wt, 8, 7)).astype(BF16)
    full = lambda shape: pl.BlockSpec(shape, lambda i: (0,) * len(shape), pipeline_mode=pl.Buffered(1))
    pair_out, logits = pl.pallas_call(
        pair_kernel,
        grid=(rows // here,),
        out_shape=(
            jax.ShapeDtypeStruct(pair_rep.shape, F32),
            jax.ShapeDtypeStruct((rows * heads, cols), F32),
        ),
        in_specs=[
            full(left_all.shape),
            full(right_all.shape),
            full(w_outer.shape),
            full((2 * heads, pair_width)),
            pl.BlockSpec((here, cols, pair_width), lambda i: (i, 0, 0)),
        ],
        out_specs=(
            pl.BlockSpec((here, cols, pair_width), lambda i: (i, 0, 0)),
            pl.BlockSpec((here * heads, cols), lambda i: (i, 0)),
        ),
        scratch_shapes=[
            pltpu.VMEM((3 * factor, factor * pair_width), BF16),
            pltpu.VMEM((n_col, rows * seqs, 3 * factor), BF16),
            pltpu.VMEM((2 * cols, n_col * k_col), BF16),
            pltpu.VMEM((8, cols), F32),
            pltpu.VMEM((here, n_col, factor // 2, 2 * seqs, pair_width), BF16),
            pltpu.VMEM((here, n_col, factor // 2, 2 * seqs, pair_width), BF16),
        ],
        compiler_params=pltpu.CompilerParams(vmem_limit_bytes=VMEM_LIMIT),
        name="pair",
    )(left_all, right_all, w_outer, jnp.concatenate([wt_high, wt_low], axis=0), pair_rep)
    alignment_out = pl.pallas_call(
        functools.partial(average_kernel, n_col),
        out_shape=jax.ShapeDtypeStruct(alignment.shape, F32),
        in_specs=[vmem] * 6,
        out_specs=vmem,
        scratch_shapes=[
            pltpu.VMEM((n_col,) + logits.shape, F32),
            dma((n_col,)),
            dma((n_col,)),
        ],
        compiler_params=pltpu.CompilerParams(
            collective_id=1, has_side_effects=True, vmem_limit_bytes=VMEM_LIMIT
        ),
        name="average",
    )(
        logits,
        norm_all.reshape(n_row * rows, seqs * width),
        alignment,
        value_weight,
        gate_weight,
        output_weight,
    )
    return (alignment_out, pair_out)


def solution(mesh):
    in_specs = (P("col", "row", None), P("row", "col", None), P("col"), P("row")) + (P(),) * 7
    out_specs = (P("col", "row", None), P("row", "col", None))
    return jax.shard_map(
        functools.partial(per_device, mesh.shape["row"], mesh.shape["col"]),
        mesh=mesh,
        in_specs=in_specs,
        out_specs=out_specs,
        check_vma=False,
    )
```

```python
import functools

import jax
import jax.numpy as jnp
from jax import lax
from jax.experimental import pallas as pl
from jax.experimental.pallas import tpu as pltpu
from jax.sharding import PartitionSpec as P

MESH = pl.DeviceIdType.MESH
F32 = jnp.float32
BF16 = jnp.bfloat16
epsilon = 1e-05
VMEM_LIMIT = 60 * 1024 * 1024


def layer_norm(values):
    center = jnp.mean(values, axis=-1, keepdims=True)
    centred = values - center
    return centred * lax.rsqrt(jnp.mean(centred * centred, axis=-1, keepdims=True) + epsilon)


def split(values):
    high = values.astype(BF16)
    return high, (values - high.astype(F32)).astype(BF16)


def dot(left, right):
    return jnp.dot(left, right, preferred_element_type=F32)


def dot_t(left, right):
    return lax.dot_general(left, right, (((1,), (1,)), ((), ())), preferred_element_type=F32)


def dot_split(left, right_high, right_low, multiply=dot):
    high, low = split(left)
    return multiply(high, right_high) + (multiply(low, right_high) + multiply(high, right_low))


def exchange_kernel(
    n_row,
    n_col,
    ratio,
    seq_ref,
    res_ref,
    align_ref,
    left_w_ref,
    right_w_ref,
    left_out,
    right_out,
    norm_buf,
    rows_buf,
    masked_buf,
    block_buf,
    left_buf,
    right_buf,
    left_send,
    left_recv,
    right_send,
    right_recv,
):
    row, col = lax.axis_index("row"), lax.axis_index("col")
    n = n_row * n_col
    me = row * n_col + col
    barrier = pltpu.get_barrier_semaphore()

    def greet(step, carry):
        other = lax.rem(me + step, n)
        pl.semaphore_signal(
            barrier,
            inc=1,
            device_id=(other // n_col, lax.rem(other, n_col)),
            device_id_type=MESH,
        )
        return carry

    lax.fori_loop(1, n, greet, 0)
    seqs, rows, width = align_ref.shape
    res_row = res_ref[...].astype(F32)
    diag = lax.broadcasted_iota(jnp.int32, (rows, rows), 0) == lax.broadcasted_iota(
        jnp.int32, (rows, rows), 1
    )
    res_col = jnp.sum(
        jnp.where(diag, jnp.broadcast_to(res_row, (rows, rows)), 0.0), axis=1, keepdims=True
    )
    factor = right_w_ref.shape[0]
    spread = jnp.broadcast_to(right_w_ref[...][:, None, :], (factor, seqs, width))
    row_seq = lax.broadcasted_iota(jnp.int32, (factor, seqs, width), 1)
    seq_sum = 0.0
    for s in range(seqs):
        normed = layer_norm(align_ref[s])
        norm_buf[:, s * width : (s + 1) * width] = normed
        live = seq_ref[s].astype(F32)
        seq_sum = seq_sum + live
        masked = normed * (res_col * live)
        masked_buf[:, s * width : (s + 1) * width] = masked
        rows_buf[pl.ds(s, rows, stride=seqs), :] = masked
        block_buf[:, s * width : (s + 1) * width] = jnp.where(row_seq == s, spread, 0.0).reshape(
            factor * seqs, width
        )
    wl_high, wl_low = split(left_w_ref[...])
    left = dot_split(rows_buf[...], wl_high, wl_low, dot_t)
    quarter = left.shape[0] // 4
    for g in range(4):
        left_buf[0:quarter, g * factor : (g + 1) * factor] = left[g * quarter : (g + 1) * quarter]
    left_buf[quarter : quarter + 8, :] = jnp.full((8, left_buf.shape[1]), seq_sum, F32)
    wr_high, wr_low = split(block_buf[...])
    right_buf[0:rows, :] = dot_split(masked_buf[...], wr_high, wr_low, dot_t)
    right_buf[rows : rows + 8, 0:rows] = jnp.broadcast_to(res_row, (8, rows))
    right_buf[rows : rows + 8, rows:] = jnp.zeros((8, right_buf.shape[1] - rows), F32)

    pl.semaphore_wait(barrier, n - 1)
    dest = row // ratio
    spot = lax.rem(row, ratio)
    started = []
    for k in range(1, n_col):
        peer = lax.rem(col + k, n_col)
        copy = pltpu.make_async_remote_copy(
            left_buf,
            left_out.at[col],
            left_send.at[k],
            left_recv.at[n_col - k],
            device_id=(row, peer),
            device_id_type=MESH,
        )
        copy.start()
        started.append(copy)
    away = dest != col
    for k in range(1, n_row):
        copy = pltpu.make_async_remote_copy(
            right_buf,
            right_out.at[spot, col],
            right_send.at[k],
            right_recv.at[spot, col],
            device_id=(lax.rem(row + k, n_row), dest),
            device_id_type=MESH,
        )
        copy.start()
    own_remote = pltpu.make_async_remote_copy(
        right_buf,
        right_out.at[spot, col],
        right_send.at[0],
        right_recv.at[spot, col],
        device_id=(row, dest),
        device_id_type=MESH,
    )
    own_local = pltpu.make_async_copy(right_buf, right_out.at[spot, col], right_recv.at[spot, col])

    @pl.when(away)
    def _():
        own_remote.start()

    @pl.when(jnp.logical_not(away))
    def _():
        own_local.start()

    left_own = pltpu.make_async_copy(left_buf, left_out.at[col], left_recv.at[0])
    left_own.start()
    left_own.wait()
    for copy in started:
        copy.wait_send()
    for k in range(1, n_row):
        pltpu.make_async_copy(right_buf, right_buf, right_send.at[k]).wait()

    @pl.when(away)
    def _():
        own_remote.wait_send()

    for k in range(1, n_col):
        src = lax.rem(col + k, n_col)
        pltpu.make_async_copy(left_buf, left_out.at[src], left_recv.at[k]).wait()
    for t in range(ratio):
        for c in range(n_col):
            pltpu.make_async_copy(right_buf, right_out.at[t, c], right_recv.at[t, c]).wait()


def pair_kernel(
    n_row,
    n_col,
    left_ref,
    right_ref,
    outer_ref,
    logits_w_ref,
    norm_ref,
    pair_ref,
    pair_out,
    slots,
    norm_out,
    w_buf,
    l_buf,
    r_buf,
    mask_buf,
    high_buf,
    low_buf,
    logits_buf,
    logits_send,
    logits_recv,
    logits_own,
    norm_send,
    norm_recv,
    relay_send,
    relay_recv,
    norm_local,
):
    row, col = lax.axis_index("row"), lax.axis_index("col")
    half = n_row // 2
    chip, core = row // 2, lax.rem(row, 2)
    partner = 2 * chip + 1 - core
    barrier = pltpu.get_barrier_semaphore()
    quarter = left_ref.shape[1] - 8
    ratio, rows = right_ref.shape[0], right_ref.shape[2] - 8
    k_col = right_ref.shape[3]
    factor = w_buf.shape[0] // 3
    here, cols, width = pair_ref.shape
    heads = logits_w_ref.shape[0]
    seqs = k_col // factor
    step = pl.program_id(0)
    steps = pl.num_programs(0)

    def peer_row(k):
        return 2 * lax.rem(chip + k, half) + core

    def norm_copy(k):
        return pltpu.make_async_remote_copy(
            norm_ref,
            norm_out.at[row],
            norm_send.at[k],
            norm_recv.at[half - k],
            device_id=(peer_row(k), col),
            device_id_type=MESH,
        )

    def relay_copy(k):
        return pltpu.make_async_remote_copy(
            norm_ref if k == 0 else norm_out.at[peer_row(k)],
            norm_out.at[peer_row(k)],
            relay_send.at[k],
            relay_recv.at[k],
            device_id=(partner, col),
            device_id_type=MESH,
        )

    own_norm = pltpu.make_async_copy(norm_ref, norm_out.at[row], norm_local)
    size = pair_ref.shape[0] * heads

    def logits_copy(k, at):
        part = pl.ds(pl.multiple_of(at * size, size), size)
        return pltpu.make_async_remote_copy(
            logits_buf.at[part],
            slots.at[col, part],
            logits_send.at[k, at],
            logits_recv.at[n_col - k, at],
            device_id=(row, lax.rem(col + k, n_col)),
            device_id_type=MESH,
        )

    def own_logits(at):
        part = pl.ds(pl.multiple_of(at * size, size), size)
        return pltpu.make_async_copy(logits_buf.at[part], slots.at[col, part], logits_own.at[at])

    @pl.when(step == 0)
    def _():
        for k in range(1, n_col):
            pl.semaphore_signal(
                barrier, inc=1, device_id=(row, lax.rem(col + k, n_col)), device_id_type=MESH
            )
        for k in range(1, half):
            pl.semaphore_signal(barrier, inc=1, device_id=(peer_row(k), col), device_id_type=MESH)
        pl.semaphore_signal(barrier, inc=1, device_id=(partner, col), device_id_type=MESH)
        own_norm.start()
        for b in range(factor):
            high, low = split(outer_ref[pl.ds(b, factor, stride=factor), :])
            lanes = slice(b * width, (b + 1) * width)
            w_buf[0:factor, lanes] = high
            w_buf[factor : 2 * factor, lanes] = low
            w_buf[2 * factor : 3 * factor, lanes] = high
        count = left_ref[0, quarter : quarter + 1, 0:1]
        for c in range(1, n_col):
            count = count + left_ref[c, quarter : quarter + 1, 0:1]
        scale = 1.0 / jnp.maximum(count, 1.0)
        for c in range(n_col):
            packed = left_ref[c, 0:quarter, :] * scale
            high = packed.astype(BF16).astype(F32)
            low = packed - high
            for g in range(4):
                lanes = slice(g * factor, (g + 1) * factor)
                parts = [high[:, lanes], high[:, lanes], low[:, lanes]]
                l_buf[c, g * quarter : (g + 1) * quarter, :] = jnp.concatenate(
                    parts, axis=1
                ).astype(BF16)
            for t in range(ratio):
                high_r, low_r = split(right_ref[t, c, 0:rows, :])
                lanes = slice(c * k_col, (c + 1) * k_col)
                r_buf[t * rows : (t + 1) * rows, lanes] = high_r
                r_buf[cols + t * rows : cols + (t + 1) * rows, lanes] = low_r
        for t in range(ratio):
            mask_buf[:, t * rows : (t + 1) * rows] = (
                right_ref[t, 0, rows : rows + 8, 0:rows] - 1.0
            ) * 1000000000.0

    group = here * seqs
    l_rows = jnp.concatenate(
        [l_buf[c, pl.ds(pl.multiple_of(step * group, group), group), :] for c in range(n_col)],
        axis=0,
    )
    for nb in range(factor // 2):
        mixed = dot(l_rows, w_buf[:, nb * 2 * width : (nb + 1) * 2 * width])
        tiles = jnp.concatenate(
            [
                mixed[:, :width].reshape(n_col * here, seqs, width),
                mixed[:, width:].reshape(n_col * here, seqs, width),
            ],
            axis=1,
        )
        high, low = split(tiles)
        for c in range(n_col):
            high_buf[:, c, nb] = high[c * here : (c + 1) * here]
            low_buf[:, c, nb] = low[c * here : (c + 1) * here]
    depth = n_col * k_col
    r_both = r_buf[...]
    w_high, w_low = split(logits_w_ref[...])
    w_both = jnp.concatenate([w_high.astype(F32), w_low.astype(F32)], axis=0).astype(BF16)
    for p in range(here // 2):
        right_high = jnp.concatenate(
            [high_buf[2 * p + t].reshape(depth, width) for t in range(2)], axis=1
        )
        right_low = jnp.concatenate(
            [low_buf[2 * p + t].reshape(depth, width) for t in range(2)], axis=1
        )
        first = dot(r_both, right_high)
        sums = first[:cols] + (first[cols:] + dot(r_both[:cols], right_low))
        for t in range(2):
            i = 2 * p + t
            pair = pair_ref[i] + sums[:, t * width : (t + 1) * width]
            pair_out[i] = pair
            high, low = split(layer_norm(pair))
            one = dot_t(w_both, high)
            two = dot_t(w_both, low)
            logits = one[:heads] + (one[heads:] + two[:heads])
            start = pl.multiple_of(step * size + i * heads, heads)
            logits_buf[pl.ds(start, heads), :] = logits + mask_buf[...]

    @pl.when(step == 0)
    def _():
        pl.semaphore_wait(barrier, n_col - 1 + half)
        relay_copy(0).start()
        for k in range(1, half):
            norm_copy(k).start()

    for k in range(1, n_col):
        logits_copy(k, step).start()
    own_logits(step).start()

    @pl.when(step == steps // 2)
    def _():
        for k in range(1, half):
            pltpu.make_async_copy(norm_ref, norm_out.at[peer_row(k)], norm_recv.at[k]).wait()
            relay_copy(k).start()

    @pl.when(step == steps - 1)
    def _():
        own_norm.wait()
        for k in range(half):
            other = 2 * lax.rem(chip + k, half) + 1 - core
            relay_copy(k).wait_send()
            pltpu.make_async_copy(norm_ref, norm_out.at[other], relay_recv.at[k]).wait()
        for k in range(1, half):
            norm_copy(k).wait_send()

        def drain(at, carry):
            own_logits(at).wait()
            part = pl.ds(pl.multiple_of(at * size, size), size)
            for k in range(1, n_col):
                logits_copy(k, at).wait_send()
                src = lax.rem(col + k, n_col)
                pltpu.make_async_copy(
                    logits_buf.at[part], slots.at[src, part], logits_recv.at[k, at]
                ).wait()
            return carry

        lax.fori_loop(0, steps, drain, 0)


def average_kernel(
    slots,
    norm_ref,
    align_ref,
    value_w_ref,
    gate_w_ref,
    output_w_ref,
    out_ref,
    terms_buf,
):
    seqs, rows, width = align_ref.shape
    n_col, total_rows, cols = slots.shape
    heads = total_rows // rows
    channels = value_w_ref.shape[1]
    head_width = channels // heads
    wv_high, wv_low = split(value_w_ref[...])
    wg_high, wg_low = split(gate_w_ref[...])
    wo_high, wo_low = split(output_w_ref[...])
    own_head = (
        lax.broadcasted_iota(jnp.int32, (heads, channels), 1) // head_width
        == lax.broadcasted_iota(jnp.int32, (heads, channels), 0)
    ).astype(F32)
    top = jnp.max(slots[0], axis=1, keepdims=True)
    for c in range(1, n_col):
        top = jnp.maximum(top, jnp.max(slots[c], axis=1, keepdims=True))
    total = jnp.zeros_like(top)
    for c in range(n_col):
        terms = jnp.exp(slots[c] - top)
        terms_buf[c] = terms
        total = total + jnp.sum(terms, axis=1, keepdims=True)
    inverse = 1.0 / total
    mixed = None
    for c in range(n_col):
        high, low = split(norm_ref[c * cols : (c + 1) * cols, :])
        part = dot_split(terms_buf[c] * inverse, high, low)
        mixed = part if mixed is None else mixed + part
    for s in range(seqs):
        wide = dot_split(mixed[:, s * width : (s + 1) * width], wv_high, wv_low)
        averaged = jnp.sum(wide.reshape(rows, heads, channels) * own_head[None], axis=1)
        align = align_ref[s]
        gate = jax.nn.sigmoid(dot_split(layer_norm(align), wg_high, wg_low))
        out_ref[s] = align + dot_split(gate * averaged, wo_high, wo_low, dot_t)


def per_device(
    n_row,
    n_col,
    alignment,
    pair_rep,
    seq_mask,
    res_mask,
    left_weight,
    right_weight,
    w_outer,
    w_logits,
    value_weight,
    gate_weight,
    output_weight,
):
    seqs, rows, width = alignment.shape
    cols, pair_width = pair_rep.shape[1], pair_rep.shape[2]
    factor = left_weight.shape[1]
    heads = w_logits.shape[1]
    ratio = cols // rows
    k_col = factor * seqs
    quarter = rows * seqs // 4
    vmem = pl.BlockSpec(memory_space=pltpu.VMEM)
    smem = pl.BlockSpec(memory_space=pltpu.SMEM)
    dma = pltpu.SemaphoreType.DMA
    left_shape = (quarter + 8, 4 * factor)
    right_shape = (rows + 8, k_col)
    norm_shape = (rows, seqs * width)
    left_all, right_all, norm_own = pl.pallas_call(
        functools.partial(exchange_kernel, n_row, n_col, ratio),
        out_shape=(
            jax.ShapeDtypeStruct((n_col,) + left_shape, F32),
            jax.ShapeDtypeStruct((ratio, n_col) + right_shape, F32),
            jax.ShapeDtypeStruct(norm_shape, F32),
        ),
        in_specs=[smem, vmem, vmem, vmem, vmem],
        out_specs=(vmem, vmem, vmem),
        scratch_shapes=[
            pltpu.VMEM((rows * seqs, width), F32),
            pltpu.VMEM(norm_shape, F32),
            pltpu.VMEM((k_col, seqs * width), F32),
            pltpu.VMEM(left_shape, F32),
            pltpu.VMEM(right_shape, F32),
            dma((n_col,)),
            dma((n_col,)),
            dma((n_row,)),
            dma((ratio, n_col)),
        ],
        compiler_params=pltpu.CompilerParams(
            collective_id=0, has_side_effects=True, vmem_limit_bytes=VMEM_LIMIT
        ),
        name="exchange",
    )(
        seq_mask,
        res_mask.reshape(1, rows),
        alignment,
        left_weight.T,
        right_weight.T,
    )
    here = 8
    steps = rows // here
    half = n_row // 2
    anywhere = pl.BlockSpec(memory_space=pl.ANY)
    full = lambda shape: pl.BlockSpec(shape, lambda i: (0,) * len(shape), pipeline_mode=pl.Buffered(1))
    pair_out, slots, norm_all = pl.pallas_call(
        functools.partial(pair_kernel, n_row, n_col),
        grid=(steps,),
        out_shape=(
            jax.ShapeDtypeStruct(pair_rep.shape, F32),
            jax.ShapeDtypeStruct((n_col, rows * heads, cols), F32),
            jax.ShapeDtypeStruct((n_row,) + norm_shape, F32),
        ),
        in_specs=[
            full(left_all.shape),
            full(right_all.shape),
            full(w_outer.shape),
            full((heads, pair_width)),
            anywhere,
            pl.BlockSpec((here, cols, pair_width), lambda i: (i, 0, 0)),
        ],
        out_specs=(
            pl.BlockSpec((here, cols, pair_width), lambda i: (i, 0, 0)),
            anywhere,
            anywhere,
        ),
        scratch_shapes=[
            pltpu.VMEM((3 * factor, factor * pair_width), BF16),
            pltpu.VMEM((n_col, rows * seqs, 3 * factor), BF16),
            pltpu.VMEM((2 * cols, n_col * k_col), BF16),
            pltpu.VMEM((8, cols), F32),
            pltpu.VMEM((here, n_col, factor // 2, 2 * seqs, pair_width), BF16),
            pltpu.VMEM((here, n_col, factor // 2, 2 * seqs, pair_width), BF16),
            pltpu.VMEM((rows * heads, cols), F32),
            dma((n_col, steps)),
            dma((n_col, steps)),
            dma((steps,)),
            dma((half,)),
            dma((half,)),
            dma((half,)),
            dma((half,)),
            dma,
        ],
        compiler_params=pltpu.CompilerParams(
            collective_id=1, has_side_effects=True, vmem_limit_bytes=VMEM_LIMIT
        ),
        name="pair",
    )(left_all, right_all, w_outer, w_logits.T, norm_own, pair_rep)
    alignment_out = pl.pallas_call(
        average_kernel,
        out_shape=jax.ShapeDtypeStruct(alignment.shape, F32),
        in_specs=[vmem] * 6,
        out_specs=vmem,
        scratch_shapes=[pltpu.VMEM(slots.shape, F32)],
        compiler_params=pltpu.CompilerParams(vmem_limit_bytes=VMEM_LIMIT),
        name="average",
    )(
        slots,
        norm_all.reshape(n_row * rows, seqs * width),
        alignment,
        value_weight,
        gate_weight,
        output_weight.T,
    )
    return (alignment_out, pair_out)


def solution(mesh):
    in_specs = (P("col", "row", None), P("row", "col", None), P("col"), P("row")) + (P(),) * 7
    out_specs = (P("col", "row", None), P("row", "col", None))
    return jax.shard_map(
        functools.partial(per_device, mesh.shape["row"], mesh.shape["col"]),
        mesh=mesh,
        in_specs=in_specs,
        out_specs=out_specs,
        check_vma=False,
    )
```

```python
import functools

import jax
import jax.numpy as jnp
from jax import lax
from jax.experimental import pallas as pl
from jax.experimental.pallas import tpu as pltpu
from jax.sharding import PartitionSpec as P

MESH = pl.DeviceIdType.MESH
F32 = jnp.float32
BF16 = jnp.bfloat16
epsilon = 1e-05
VMEM_LIMIT = 60 * 1024 * 1024


def layer_norm(values):
    center = jnp.mean(values, axis=-1, keepdims=True)
    centred = values - center
    return centred * lax.rsqrt(jnp.mean(centred * centred, axis=-1, keepdims=True) + epsilon)


def split(values):
    high = values.astype(BF16)
    return high, (values - high.astype(F32)).astype(BF16)


def dot(left, right):
    return jnp.dot(left, right, preferred_element_type=F32)


def dot_t(left, right):
    return lax.dot_general(left, right, (((1,), (1,)), ((), ())), preferred_element_type=F32)


def dot_split(left, right_high, right_low, multiply=dot):
    high, low = split(left)
    return multiply(high, right_high) + (multiply(low, right_high) + multiply(high, right_low))


def exchange_kernel(
    n_row,
    n_col,
    ratio,
    seq_ref,
    res_ref,
    align_ref,
    left_w_ref,
    right_w_ref,
    left_out,
    right_out,
    norm_buf,
    rows_buf,
    masked_buf,
    block_buf,
    left_buf,
    right_buf,
    left_send,
    left_recv,
    turn_sem,
    right_send,
    right_recv,
    relay_send,
    relay_recv,
):
    row, col = lax.axis_index("row"), lax.axis_index("col")
    n = n_row * n_col
    me = row * n_col + col
    barrier = pltpu.get_barrier_semaphore()

    def greet(step, carry):
        other = lax.rem(me + step, n)
        pl.semaphore_signal(
            barrier,
            inc=1,
            device_id=(other // n_col, lax.rem(other, n_col)),
            device_id_type=MESH,
        )
        return carry

    lax.fori_loop(1, n, greet, 0)
    seqs, rows, width = align_ref.shape
    res_row = res_ref[...].astype(F32)
    diag = lax.broadcasted_iota(jnp.int32, (rows, rows), 0) == lax.broadcasted_iota(
        jnp.int32, (rows, rows), 1
    )
    res_col = jnp.sum(
        jnp.where(diag, jnp.broadcast_to(res_row, (rows, rows)), 0.0), axis=1, keepdims=True
    )
    factor = right_w_ref.shape[0]
    spread = jnp.broadcast_to(right_w_ref[...][:, None, :], (factor, seqs, width))
    row_seq = lax.broadcasted_iota(jnp.int32, (factor, seqs, width), 1)
    seq_sum = 0.0
    for s in range(seqs):
        normed = layer_norm(align_ref[s])
        norm_buf[:, s * width : (s + 1) * width] = normed
        live = seq_ref[s].astype(F32)
        seq_sum = seq_sum + live
        masked = normed * (res_col * live)
        masked_buf[:, s * width : (s + 1) * width] = masked
        rows_buf[pl.ds(s, rows, stride=seqs), :] = masked
        block_buf[:, s * width : (s + 1) * width] = jnp.where(row_seq == s, spread, 0.0).reshape(
            factor * seqs, width
        )
    wl_high, wl_low = split(left_w_ref[...])
    left = dot_split(rows_buf[...], wl_high, wl_low, dot_t)
    quarter = left.shape[0] // 4
    for g in range(4):
        left_buf[0:quarter, g * factor : (g + 1) * factor] = left[g * quarter : (g + 1) * quarter]
    left_buf[quarter : quarter + 8, :] = jnp.full((8, left_buf.shape[1]), seq_sum, F32)
    wr_high, wr_low = split(block_buf[...])
    right_buf[0:rows, :] = dot_split(masked_buf[...], wr_high, wr_low, dot_t)
    right_buf[rows : rows + 8, 0:rows] = jnp.broadcast_to(res_row, (8, rows))
    right_buf[rows : rows + 8, rows:] = jnp.zeros((8, right_buf.shape[1] - rows), F32)

    pl.semaphore_wait(barrier, n - 1)
    dest = row // ratio
    spot = col * ratio + lax.rem(row, ratio)
    away = dest != col
    half = n_row // 2
    chip, core = row // 2, lax.rem(row, 2)
    partner = 2 * chip + 1 - core

    def peer_row(k):
        return 2 * lax.rem(chip + k, half) + core

    turn = pltpu.make_async_remote_copy(
        right_buf,
        right_out.at[spot],
        turn_sem.at[0],
        turn_sem.at[1],
        device_id=(spot, dest),
        device_id_type=MESH,
    )
    stay = pltpu.make_async_copy(right_buf, right_out.at[spot], turn_sem.at[1])

    @pl.when(away)
    def _():
        turn.start()

    @pl.when(jnp.logical_not(away))
    def _():
        stay.start()

    started = []
    for k in range(1, n_col):
        copy = pltpu.make_async_remote_copy(
            left_buf,
            left_out.at[col],
            left_send.at[k],
            left_recv.at[n_col - k],
            device_id=(row, lax.rem(col + k, n_col)),
            device_id_type=MESH,
        )
        copy.start()
        started.append(copy)
    left_own = pltpu.make_async_copy(left_buf, left_out.at[col], left_recv.at[0])
    left_own.start()
    pltpu.make_async_copy(right_buf, right_out.at[row], turn_sem.at[1]).wait()
    for k in range(1, half):
        copy = pltpu.make_async_remote_copy(
            right_out.at[row],
            right_out.at[row],
            right_send.at[k],
            right_recv.at[half - k],
            device_id=(peer_row(k), col),
            device_id_type=MESH,
        )
        copy.start()
        started.append(copy)
    for k in range(half):
        src = peer_row(k)
        if k > 0:
            pltpu.make_async_copy(right_buf, right_out.at[src], right_recv.at[k]).wait()
        copy = pltpu.make_async_remote_copy(
            right_out.at[src],
            right_out.at[src],
            relay_send.at[k],
            relay_recv.at[k],
            device_id=(partner, col),
            device_id_type=MESH,
        )
        copy.start()
        started.append(copy)
    left_own.wait()
    for k in range(1, n_col):
        src = lax.rem(col + k, n_col)
        pltpu.make_async_copy(left_buf, left_out.at[src], left_recv.at[k]).wait()
    for k in range(half):
        src = 2 * lax.rem(chip + k, half) + 1 - core
        pltpu.make_async_copy(right_buf, right_out.at[src], relay_recv.at[k]).wait()
    for copy in started:
        copy.wait_send()

    @pl.when(away)
    def _():
        turn.wait_send()


def pair_kernel(
    n_row,
    n_col,
    left_ref,
    right_ref,
    outer_ref,
    logits_w_ref,
    norm_ref,
    pair_ref,
    pair_out,
    slots,
    norm_out,
    w_buf,
    l_buf,
    r_buf,
    mask_buf,
    high_buf,
    low_buf,
    logits_buf,
    logits_send,
    logits_recv,
    logits_own,
    norm_send,
    norm_recv,
    relay_send,
    relay_recv,
    norm_local,
):
    row, col = lax.axis_index("row"), lax.axis_index("col")
    half = n_row // 2
    chip, core = row // 2, lax.rem(row, 2)
    partner = 2 * chip + 1 - core
    barrier = pltpu.get_barrier_semaphore()
    quarter = left_ref.shape[1] - 8
    ratio, rows = n_row // n_col, right_ref.shape[1] - 8
    k_col = right_ref.shape[2]
    factor = w_buf.shape[0] // 3
    here, cols, width = pair_ref.shape
    heads = logits_w_ref.shape[0]
    seqs = k_col // factor
    step = pl.program_id(0)
    steps = pl.num_programs(0)

    def peer_row(k):
        return 2 * lax.rem(chip + k, half) + core

    def norm_copy(k):
        return pltpu.make_async_remote_copy(
            norm_ref,
            norm_out.at[row],
            norm_send.at[k],
            norm_recv.at[half - k],
            device_id=(peer_row(k), col),
            device_id_type=MESH,
        )

    def relay_copy(k):
        return pltpu.make_async_remote_copy(
            norm_ref if k == 0 else norm_out.at[peer_row(k)],
            norm_out.at[peer_row(k)],
            relay_send.at[k],
            relay_recv.at[k],
            device_id=(partner, col),
            device_id_type=MESH,
        )

    own_norm = pltpu.make_async_copy(norm_ref, norm_out.at[row], norm_local)
    size = pair_ref.shape[0] * heads

    def logits_copy(k, at):
        part = pl.ds(pl.multiple_of(at * size, size), size)
        return pltpu.make_async_remote_copy(
            logits_buf.at[part],
            slots.at[col, part],
            logits_send.at[k, at],
            logits_recv.at[n_col - k, at],
            device_id=(row, lax.rem(col + k, n_col)),
            device_id_type=MESH,
        )

    def own_logits(at):
        part = pl.ds(pl.multiple_of(at * size, size), size)
        return pltpu.make_async_copy(logits_buf.at[part], slots.at[col, part], logits_own.at[at])

    @pl.when(step == 0)
    def _():
        for k in range(1, n_col):
            pl.semaphore_signal(
                barrier, inc=1, device_id=(row, lax.rem(col + k, n_col)), device_id_type=MESH
            )
        for k in range(1, half):
            pl.semaphore_signal(barrier, inc=1, device_id=(peer_row(k), col), device_id_type=MESH)
        pl.semaphore_signal(barrier, inc=1, device_id=(partner, col), device_id_type=MESH)
        own_norm.start()
        for b in range(factor):
            high, low = split(outer_ref[pl.ds(b, factor, stride=factor), :])
            lanes = slice(b * width, (b + 1) * width)
            w_buf[0:factor, lanes] = high
            w_buf[factor : 2 * factor, lanes] = low
            w_buf[2 * factor : 3 * factor, lanes] = high
        count = left_ref[0, quarter : quarter + 1, 0:1]
        for c in range(1, n_col):
            count = count + left_ref[c, quarter : quarter + 1, 0:1]
        scale = 1.0 / jnp.maximum(count, 1.0)
        for c in range(n_col):
            packed = left_ref[c, 0:quarter, :] * scale
            high = packed.astype(BF16).astype(F32)
            low = packed - high
            for g in range(4):
                lanes = slice(g * factor, (g + 1) * factor)
                parts = [high[:, lanes], high[:, lanes], low[:, lanes]]
                l_buf[c, g * quarter : (g + 1) * quarter, :] = jnp.concatenate(
                    parts, axis=1
                ).astype(BF16)
            for t in range(ratio):
                high_r, low_r = split(right_ref[c * ratio + t, 0:rows, :])
                lanes = slice(c * k_col, (c + 1) * k_col)
                r_buf[t * rows : (t + 1) * rows, lanes] = high_r
                r_buf[cols + t * rows : cols + (t + 1) * rows, lanes] = low_r
        for t in range(ratio):
            mask_buf[:, t * rows : (t + 1) * rows] = (
                right_ref[t, rows : rows + 8, 0:rows] - 1.0
            ) * 1000000000.0

    group = here * seqs
    l_rows = jnp.concatenate(
        [l_buf[c, pl.ds(pl.multiple_of(step * group, group), group), :] for c in range(n_col)],
        axis=0,
    )
    for nb in range(factor // 2):
        mixed = dot(l_rows, w_buf[:, nb * 2 * width : (nb + 1) * 2 * width])
        tiles = jnp.concatenate(
            [
                mixed[:, :width].reshape(n_col * here, seqs, width),
                mixed[:, width:].reshape(n_col * here, seqs, width),
            ],
            axis=1,
        )
        high, low = split(tiles)
        for c in range(n_col):
            high_buf[:, c, nb] = high[c * here : (c + 1) * here]
            low_buf[:, c, nb] = low[c * here : (c + 1) * here]
    depth = n_col * k_col
    r_both = r_buf[...]
    w_high, w_low = split(logits_w_ref[...])
    w_both = jnp.concatenate([w_high.astype(F32), w_low.astype(F32)], axis=0).astype(BF16)
    for p in range(here // 2):
        right_high = jnp.concatenate(
            [high_buf[2 * p + t].reshape(depth, width) for t in range(2)], axis=1
        )
        right_low = jnp.concatenate(
            [low_buf[2 * p + t].reshape(depth, width) for t in range(2)], axis=1
        )
        first = dot(r_both, right_high)
        sums = first[:cols] + (first[cols:] + dot(r_both[:cols], right_low))
        for t in range(2):
            i = 2 * p + t
            pair = pair_ref[i] + sums[:, t * width : (t + 1) * width]
            pair_out[i] = pair
            high, low = split(layer_norm(pair))
            one = dot_t(w_both, high)
            two = dot_t(w_both, low)
            logits = one[:heads] + (one[heads:] + two[:heads])
            start = pl.multiple_of(step * size + i * heads, heads)
            logits_buf[pl.ds(start, heads), :] = logits + mask_buf[...]

    @pl.when(step == 0)
    def _():
        pl.semaphore_wait(barrier, n_col - 1 + half)
        relay_copy(0).start()
        for k in range(1, half):
            norm_copy(k).start()

    for k in range(1, n_col):
        logits_copy(k, step).start()
    own_logits(step).start()

    @pl.when(step == steps // 2)
    def _():
        for k in range(1, half):
            pltpu.make_async_copy(norm_ref, norm_out.at[peer_row(k)], norm_recv.at[k]).wait()
            relay_copy(k).start()

    @pl.when(step == steps - 1)
    def _():
        own_norm.wait()
        for k in range(half):
            other = 2 * lax.rem(chip + k, half) + 1 - core
            relay_copy(k).wait_send()
            pltpu.make_async_copy(norm_ref, norm_out.at[other], relay_recv.at[k]).wait()
        for k in range(1, half):
            norm_copy(k).wait_send()

        def drain(at, carry):
            own_logits(at).wait()
            part = pl.ds(pl.multiple_of(at * size, size), size)
            for k in range(1, n_col):
                logits_copy(k, at).wait_send()
                src = lax.rem(col + k, n_col)
                pltpu.make_async_copy(
                    logits_buf.at[part], slots.at[src, part], logits_recv.at[k, at]
                ).wait()
            return carry

        lax.fori_loop(0, steps, drain, 0)


def average_kernel(
    slots,
    norm_ref,
    align_ref,
    value_w_ref,
    gate_w_ref,
    output_w_ref,
    out_ref,
    terms_buf,
):
    seqs, rows, width = align_ref.shape
    n_col, total_rows, cols = slots.shape
    heads = total_rows // rows
    channels = value_w_ref.shape[1]
    head_width = channels // heads
    wv_high, wv_low = split(value_w_ref[...])
    wg_high, wg_low = split(gate_w_ref[...])
    wo_high, wo_low = split(output_w_ref[...])
    own_head = (
        lax.broadcasted_iota(jnp.int32, (heads, channels), 1) // head_width
        == lax.broadcasted_iota(jnp.int32, (heads, channels), 0)
    ).astype(F32)
    top = jnp.max(slots[0], axis=1, keepdims=True)
    for c in range(1, n_col):
        top = jnp.maximum(top, jnp.max(slots[c], axis=1, keepdims=True))
    total = jnp.zeros_like(top)
    for c in range(n_col):
        terms = jnp.exp(slots[c] - top)
        terms_buf[c] = terms
        total = total + jnp.sum(terms, axis=1, keepdims=True)
    inverse = 1.0 / total
    mixed = None
    for c in range(n_col):
        high, low = split(norm_ref[c * cols : (c + 1) * cols, :])
        part = dot_split(terms_buf[c] * inverse, high, low)
        mixed = part if mixed is None else mixed + part
    for s in range(seqs):
        wide = dot_split(mixed[:, s * width : (s + 1) * width], wv_high, wv_low)
        averaged = jnp.sum(wide.reshape(rows, heads, channels) * own_head[None], axis=1)
        align = align_ref[s]
        gate = jax.nn.sigmoid(dot_split(layer_norm(align), wg_high, wg_low))
        out_ref[s] = align + dot_split(gate * averaged, wo_high, wo_low, dot_t)


def per_device(
    n_row,
    n_col,
    alignment,
    pair_rep,
    seq_mask,
    res_mask,
    left_weight,
    right_weight,
    w_outer,
    w_logits,
    value_weight,
    gate_weight,
    output_weight,
):
    seqs, rows, width = alignment.shape
    cols, pair_width = pair_rep.shape[1], pair_rep.shape[2]
    factor = left_weight.shape[1]
    heads = w_logits.shape[1]
    ratio = cols // rows
    k_col = factor * seqs
    quarter = rows * seqs // 4
    half = n_row // 2
    vmem = pl.BlockSpec(memory_space=pltpu.VMEM)
    smem = pl.BlockSpec(memory_space=pltpu.SMEM)
    dma = pltpu.SemaphoreType.DMA
    left_shape = (quarter + 8, 4 * factor)
    right_shape = (rows + 8, k_col)
    norm_shape = (rows, seqs * width)
    left_all, right_all, norm_own = pl.pallas_call(
        functools.partial(exchange_kernel, n_row, n_col, ratio),
        out_shape=(
            jax.ShapeDtypeStruct((n_col,) + left_shape, F32),
            jax.ShapeDtypeStruct((n_row,) + right_shape, F32),
            jax.ShapeDtypeStruct(norm_shape, F32),
        ),
        in_specs=[smem, vmem, vmem, vmem, vmem],
        out_specs=(vmem, vmem, vmem),
        scratch_shapes=[
            pltpu.VMEM((rows * seqs, width), F32),
            pltpu.VMEM(norm_shape, F32),
            pltpu.VMEM((k_col, seqs * width), F32),
            pltpu.VMEM(left_shape, F32),
            pltpu.VMEM(right_shape, F32),
            dma((n_col,)),
            dma((n_col,)),
            dma((2,)),
            dma((half,)),
            dma((half,)),
            dma((half,)),
            dma((half,)),
        ],
        compiler_params=pltpu.CompilerParams(
            collective_id=0, has_side_effects=True, vmem_limit_bytes=VMEM_LIMIT
        ),
        name="exchange",
    )(
        seq_mask,
        res_mask.reshape(1, rows),
        alignment,
        left_weight.T,
        right_weight.T,
    )
    here = 8
    steps = rows // here
    anywhere = pl.BlockSpec(memory_space=pl.ANY)
    full = lambda shape: pl.BlockSpec(shape, lambda i: (0,) * len(shape), pipeline_mode=pl.Buffered(1))
    pair_out, slots, norm_all = pl.pallas_call(
        functools.partial(pair_kernel, n_row, n_col),
        grid=(steps,),
        out_shape=(
            jax.ShapeDtypeStruct(pair_rep.shape, F32),
            jax.ShapeDtypeStruct((n_col, rows * heads, cols), F32),
            jax.ShapeDtypeStruct((n_row,) + norm_shape, F32),
        ),
        in_specs=[
            full(left_all.shape),
            full(right_all.shape),
            full(w_outer.shape),
            full((heads, pair_width)),
            anywhere,
            pl.BlockSpec((here, cols, pair_width), lambda i: (i, 0, 0)),
        ],
        out_specs=(
            pl.BlockSpec((here, cols, pair_width), lambda i: (i, 0, 0)),
            anywhere,
            anywhere,
        ),
        scratch_shapes=[
            pltpu.VMEM((3 * factor, factor * pair_width), BF16),
            pltpu.VMEM((n_col, rows * seqs, 3 * factor), BF16),
            pltpu.VMEM((2 * cols, n_col * k_col), BF16),
            pltpu.VMEM((8, cols), F32),
            pltpu.VMEM((here, n_col, factor // 2, 2 * seqs, pair_width), BF16),
            pltpu.VMEM((here, n_col, factor // 2, 2 * seqs, pair_width), BF16),
            pltpu.VMEM((rows * heads, cols), F32),
            dma((n_col, steps)),
            dma((n_col, steps)),
            dma((steps,)),
            dma((half,)),
            dma((half,)),
            dma((half,)),
            dma((half,)),
            dma,
        ],
        compiler_params=pltpu.CompilerParams(
            collective_id=1, has_side_effects=True, vmem_limit_bytes=VMEM_LIMIT
        ),
        name="pair",
    )(left_all, right_all, w_outer, w_logits.T, norm_own, pair_rep)
    alignment_out = pl.pallas_call(
        average_kernel,
        out_shape=jax.ShapeDtypeStruct(alignment.shape, F32),
        in_specs=[vmem] * 6,
        out_specs=vmem,
        scratch_shapes=[pltpu.VMEM(slots.shape, F32)],
        compiler_params=pltpu.CompilerParams(vmem_limit_bytes=VMEM_LIMIT),
        name="average",
    )(
        slots,
        norm_all.reshape(n_row * rows, seqs * width),
        alignment,
        value_weight,
        gate_weight,
        output_weight.T,
    )
    return (alignment_out, pair_out)


def solution(mesh):
    in_specs = (P("col", "row", None), P("row", "col", None), P("col"), P("row")) + (P(),) * 7
    out_specs = (P("col", "row", None), P("row", "col", None))
    return jax.shard_map(
        functools.partial(per_device, mesh.shape["row"], mesh.shape["col"]),
        mesh=mesh,
        in_specs=in_specs,
        out_specs=out_specs,
        check_vma=False,
    )
```

```python
import functools

import jax
import jax.numpy as jnp
from jax import lax
from jax.experimental import pallas as pl
from jax.experimental.pallas import tpu as pltpu
from jax.sharding import PartitionSpec as P

MESH = pl.DeviceIdType.MESH
F32 = jnp.float32
BF16 = jnp.bfloat16
epsilon = 1e-05
VMEM_LIMIT = 60 * 1024 * 1024


def layer_norm(values):
    center = jnp.mean(values, axis=-1, keepdims=True)
    centred = values - center
    return centred * lax.rsqrt(jnp.mean(centred * centred, axis=-1, keepdims=True) + epsilon)


def split(values):
    high = values.astype(BF16)
    return high, (values - high.astype(F32)).astype(BF16)


def dot(left, right):
    return jnp.dot(left, right, preferred_element_type=F32)


def dot_t(left, right):
    return lax.dot_general(left, right, (((1,), (1,)), ((), ())), preferred_element_type=F32)


def dot_split(left, right_high, right_low, multiply=dot):
    high, low = split(left)
    return multiply(high, right_high) + (multiply(low, right_high) + multiply(high, right_low))


def exchange(
    n_row,
    n_col,
    ratio,
    between,
    seq_ref,
    res_ref,
    align_ref,
    left_w_ref,
    right_w_ref,
    left_out,
    right_out,
    norm_buf,
    rows_buf,
    masked_buf,
    block_buf,
    left_buf,
    right_buf,
    left_send,
    left_recv,
    turn_sem,
    right_send,
    right_recv,
    relay_send,
    relay_recv,
):
    row, col = lax.axis_index("row"), lax.axis_index("col")
    n = n_row * n_col
    me = row * n_col + col
    barrier = pltpu.get_barrier_semaphore()

    def greet(step, carry):
        other = lax.rem(me + step, n)
        pl.semaphore_signal(
            barrier,
            inc=1,
            device_id=(other // n_col, lax.rem(other, n_col)),
            device_id_type=MESH,
        )
        return carry

    lax.fori_loop(1, n, greet, 0)
    seqs, rows, width = align_ref.shape
    res_row = res_ref[...].astype(F32)
    diag = lax.broadcasted_iota(jnp.int32, (rows, rows), 0) == lax.broadcasted_iota(
        jnp.int32, (rows, rows), 1
    )
    res_col = jnp.sum(
        jnp.where(diag, jnp.broadcast_to(res_row, (rows, rows)), 0.0), axis=1, keepdims=True
    )
    factor = right_w_ref.shape[0]
    spread = jnp.broadcast_to(right_w_ref[...][:, None, :], (factor, seqs, width))
    row_seq = lax.broadcasted_iota(jnp.int32, (factor, seqs, width), 1)
    seq_sum = 0.0
    for s in range(seqs):
        normed = layer_norm(align_ref[s])
        norm_buf[:, s * width : (s + 1) * width] = normed
        live = seq_ref[s].astype(F32)
        seq_sum = seq_sum + live
        masked = normed * (res_col * live)
        masked_buf[:, s * width : (s + 1) * width] = masked
        rows_buf[pl.ds(s, rows, stride=seqs), :] = masked
        block_buf[:, s * width : (s + 1) * width] = jnp.where(row_seq == s, spread, 0.0).reshape(
            factor * seqs, width
        )
    wl_high, wl_low = split(left_w_ref[...])
    left = dot_split(rows_buf[...], wl_high, wl_low, dot_t)
    quarter = left.shape[0] // 4
    for g in range(4):
        left_buf[0:quarter, g * factor : (g + 1) * factor] = left[g * quarter : (g + 1) * quarter]
    left_buf[quarter : quarter + 8, :] = jnp.full((8, left_buf.shape[1]), seq_sum, F32)
    wr_high, wr_low = split(block_buf[...])
    right_buf[0:rows, :] = dot_split(masked_buf[...], wr_high, wr_low, dot_t)
    right_buf[rows : rows + 8, 0:rows] = jnp.broadcast_to(res_row, (8, rows))
    right_buf[rows : rows + 8, rows:] = jnp.zeros((8, right_buf.shape[1] - rows), F32)

    pl.semaphore_wait(barrier, n - 1)
    dest = row // ratio
    spot = col * ratio + lax.rem(row, ratio)
    away = dest != col
    half = n_row // 2
    chip, core = row // 2, lax.rem(row, 2)
    partner = 2 * chip + 1 - core

    def peer_row(k):
        return 2 * lax.rem(chip + k, half) + core

    turn = pltpu.make_async_remote_copy(
        right_buf,
        right_out.at[spot],
        turn_sem.at[0],
        turn_sem.at[1],
        device_id=(spot, dest),
        device_id_type=MESH,
    )
    stay = pltpu.make_async_copy(right_buf, right_out.at[spot], turn_sem.at[1])

    @pl.when(away)
    def _():
        turn.start()

    @pl.when(jnp.logical_not(away))
    def _():
        stay.start()

    started = []
    for k in range(1, n_col):
        copy = pltpu.make_async_remote_copy(
            left_buf,
            left_out.at[col],
            left_send.at[k],
            left_recv.at[n_col - k],
            device_id=(row, lax.rem(col + k, n_col)),
            device_id_type=MESH,
        )
        copy.start()
        started.append(copy)
    left_own = pltpu.make_async_copy(left_buf, left_out.at[col], left_recv.at[0])
    left_own.start()
    between()
    pltpu.make_async_copy(right_buf, right_out.at[row], turn_sem.at[1]).wait()
    for k in range(1, half):
        copy = pltpu.make_async_remote_copy(
            right_out.at[row],
            right_out.at[row],
            right_send.at[k],
            right_recv.at[half - k],
            device_id=(peer_row(k), col),
            device_id_type=MESH,
        )
        copy.start()
        started.append(copy)
    for k in range(half):
        src = peer_row(k)
        if k > 0:
            pltpu.make_async_copy(right_buf, right_out.at[src], right_recv.at[k]).wait()
        copy = pltpu.make_async_remote_copy(
            right_out.at[src],
            right_out.at[src],
            relay_send.at[k],
            relay_recv.at[k],
            device_id=(partner, col),
            device_id_type=MESH,
        )
        copy.start()
        started.append(copy)
    left_own.wait()
    for k in range(1, n_col):
        src = lax.rem(col + k, n_col)
        pltpu.make_async_copy(left_buf, left_out.at[src], left_recv.at[k]).wait()
    for k in range(half):
        src = 2 * lax.rem(chip + k, half) + 1 - core
        pltpu.make_async_copy(right_buf, right_out.at[src], relay_recv.at[k]).wait()
    for copy in started:
        copy.wait_send()

    @pl.when(away)
    def _():
        turn.wait_send()


def pair_kernel(
    n_row,
    n_col,
    seq_ref,
    res_ref,
    align_ref,
    left_w_ref,
    right_w_ref,
    outer_ref,
    logits_w_ref,
    pair_ref,
    pair_out,
    slots,
    norm_out,
    w_buf,
    l_buf,
    r_buf,
    mask_buf,
    high_buf,
    low_buf,
    logits_buf,
    logits_send,
    logits_recv,
    logits_own,
    norm_send,
    norm_recv,
    relay_send,
    relay_recv,
    norm_local,
    left_ref,
    right_ref,
    norm_ref,
    *exchange_scratch,
):
    row, col = lax.axis_index("row"), lax.axis_index("col")
    half = n_row // 2
    chip, core = row // 2, lax.rem(row, 2)
    partner = 2 * chip + 1 - core
    quarter = left_ref.shape[1] - 8
    ratio, rows = n_row // n_col, right_ref.shape[1] - 8
    k_col = right_ref.shape[2]
    factor = w_buf.shape[0] // 3
    here, cols, width = pair_ref.shape
    heads = logits_w_ref.shape[0]
    seqs = k_col // factor
    step = pl.program_id(0)
    steps = pl.num_programs(0)

    def peer_row(k):
        return 2 * lax.rem(chip + k, half) + core

    def norm_copy(k):
        return pltpu.make_async_remote_copy(
            norm_ref,
            norm_out.at[row],
            norm_send.at[k],
            norm_recv.at[half - k],
            device_id=(peer_row(k), col),
            device_id_type=MESH,
        )

    def relay_copy(k):
        return pltpu.make_async_remote_copy(
            norm_ref if k == 0 else norm_out.at[peer_row(k)],
            norm_out.at[peer_row(k)],
            relay_send.at[k],
            relay_recv.at[k],
            device_id=(partner, col),
            device_id_type=MESH,
        )

    own_norm = pltpu.make_async_copy(norm_ref, norm_out.at[row], norm_local)
    size = pair_ref.shape[0] * heads

    def logits_copy(k, at):
        part = pl.ds(pl.multiple_of(at * size, size), size)
        return pltpu.make_async_remote_copy(
            logits_buf.at[part],
            slots.at[col, part],
            logits_send.at[k, at],
            logits_recv.at[n_col - k, at],
            device_id=(row, lax.rem(col + k, n_col)),
            device_id_type=MESH,
        )

    def own_logits(at):
        part = pl.ds(pl.multiple_of(at * size, size), size)
        return pltpu.make_async_copy(logits_buf.at[part], slots.at[col, part], logits_own.at[at])

    @pl.when(step == 0)
    def _():
        def between():
            for b in range(factor):
                high, low = split(outer_ref[pl.ds(b, factor, stride=factor), :])
                lanes = slice(b * width, (b + 1) * width)
                w_buf[0:factor, lanes] = high
                w_buf[factor : 2 * factor, lanes] = low
                w_buf[2 * factor : 3 * factor, lanes] = high

        exchange(
            n_row,
            n_col,
            ratio,
            between,
            seq_ref,
            res_ref,
            align_ref,
            left_w_ref,
            right_w_ref,
            left_ref,
            right_ref,
            norm_ref,
            *exchange_scratch,
        )
        own_norm.start()
        count = left_ref[0, quarter : quarter + 1, 0:1]
        for c in range(1, n_col):
            count = count + left_ref[c, quarter : quarter + 1, 0:1]
        scale = 1.0 / jnp.maximum(count, 1.0)
        for c in range(n_col):
            packed = left_ref[c, 0:quarter, :] * scale
            high = packed.astype(BF16).astype(F32)
            low = packed - high
            for g in range(4):
                lanes = slice(g * factor, (g + 1) * factor)
                parts = [high[:, lanes], high[:, lanes], low[:, lanes]]
                l_buf[c, g * quarter : (g + 1) * quarter, :] = jnp.concatenate(
                    parts, axis=1
                ).astype(BF16)
            for t in range(ratio):
                high_r, low_r = split(right_ref[c * ratio + t, 0:rows, :])
                lanes = slice(c * k_col, (c + 1) * k_col)
                r_buf[t * rows : (t + 1) * rows, lanes] = high_r
                r_buf[cols + t * rows : cols + (t + 1) * rows, lanes] = low_r
        for t in range(ratio):
            mask_buf[:, t * rows : (t + 1) * rows] = (
                right_ref[t, rows : rows + 8, 0:rows] - 1.0
            ) * 1000000000.0

    group = here * seqs
    l_rows = jnp.concatenate(
        [l_buf[c, pl.ds(pl.multiple_of(step * group, group), group), :] for c in range(n_col)],
        axis=0,
    )
    for nb in range(factor // 2):
        mixed = dot(l_rows, w_buf[:, nb * 2 * width : (nb + 1) * 2 * width])
        tiles = jnp.concatenate(
            [
                mixed[:, :width].reshape(n_col * here, seqs, width),
                mixed[:, width:].reshape(n_col * here, seqs, width),
            ],
            axis=1,
        )
        high, low = split(tiles)
        for c in range(n_col):
            high_buf[:, c, nb] = high[c * here : (c + 1) * here]
            low_buf[:, c, nb] = low[c * here : (c + 1) * here]
    depth = n_col * k_col
    r_both = r_buf[...]
    w_high, w_low = split(logits_w_ref[...])
    w_both = jnp.concatenate([w_high.astype(F32), w_low.astype(F32)], axis=0).astype(BF16)
    for p in range(here // 2):
        right_high = jnp.concatenate(
            [high_buf[2 * p + t].reshape(depth, width) for t in range(2)], axis=1
        )
        right_low = jnp.concatenate(
            [low_buf[2 * p + t].reshape(depth, width) for t in range(2)], axis=1
        )
        first = dot(r_both, right_high)
        sums = first[:cols] + (first[cols:] + dot(r_both[:cols], right_low))
        for t in range(2):
            i = 2 * p + t
            pair_out[i] = pair_ref[i] + sums[:, t * width : (t + 1) * width]
    batch = here // 2
    for g in range(0, here, batch):
        pairs = pair_out[g : g + batch].reshape(batch * cols, width)
        high, low = split(layer_norm(pairs))
        for t in range(batch):
            one = dot_t(w_both, high[t * cols : (t + 1) * cols])
            two = dot_t(w_both, low[t * cols : (t + 1) * cols])
            logits = one[:heads] + (one[heads:] + two[:heads])
            start = pl.multiple_of(step * size + (g + t) * heads, heads)
            logits_buf[pl.ds(start, heads), :] = logits + mask_buf[...]

    @pl.when(step == 0)
    def _():
        relay_copy(0).start()
        for k in range(1, half):
            norm_copy(k).start()

    for k in range(1, n_col):
        logits_copy(k, step).start()
    own_logits(step).start()

    @pl.when(step == steps // 2)
    def _():
        for k in range(1, half):
            pltpu.make_async_copy(norm_ref, norm_out.at[peer_row(k)], norm_recv.at[k]).wait()
            relay_copy(k).start()

    @pl.when(step == steps - 1)
    def _():
        own_norm.wait()
        for k in range(half):
            other = 2 * lax.rem(chip + k, half) + 1 - core
            relay_copy(k).wait_send()
            pltpu.make_async_copy(norm_ref, norm_out.at[other], relay_recv.at[k]).wait()
        for k in range(1, half):
            norm_copy(k).wait_send()

        def drain(at, carry):
            own_logits(at).wait()
            part = pl.ds(pl.multiple_of(at * size, size), size)
            for k in range(1, n_col):
                logits_copy(k, at).wait_send()
                src = lax.rem(col + k, n_col)
                pltpu.make_async_copy(
                    logits_buf.at[part], slots.at[src, part], logits_recv.at[k, at]
                ).wait()
            return carry

        lax.fori_loop(0, steps, drain, 0)


def average_kernel(
    slots,
    norm_ref,
    align_ref,
    value_w_ref,
    gate_w_ref,
    output_w_ref,
    out_ref,
    terms_buf,
):
    seqs, rows, width = align_ref.shape
    n_col, total_rows, cols = slots.shape
    heads = total_rows // rows
    channels = value_w_ref.shape[1]
    head_width = channels // heads
    wv_high, wv_low = split(value_w_ref[...])
    wg_high, wg_low = split(gate_w_ref[...])
    wo_high, wo_low = split(output_w_ref[...])
    own_head = (
        lax.broadcasted_iota(jnp.int32, (heads, channels), 1) // head_width
        == lax.broadcasted_iota(jnp.int32, (heads, channels), 0)
    ).astype(F32)
    top = jnp.max(slots[0], axis=1, keepdims=True)
    for c in range(1, n_col):
        top = jnp.maximum(top, jnp.max(slots[c], axis=1, keepdims=True))
    total = jnp.zeros_like(top)
    for c in range(n_col):
        terms = jnp.exp(slots[c] - top)
        terms_buf[c] = terms
        total = total + jnp.sum(terms, axis=1, keepdims=True)
    inverse = 1.0 / total
    mixed = None
    for c in range(n_col):
        high, low = split(norm_ref[c * cols : (c + 1) * cols, :])
        part = dot_split(terms_buf[c] * inverse, high, low)
        mixed = part if mixed is None else mixed + part
    for s in range(seqs):
        wide = dot_split(mixed[:, s * width : (s + 1) * width], wv_high, wv_low)
        averaged = jnp.sum(wide.reshape(rows, heads, channels) * own_head[None], axis=1)
        align = align_ref[s]
        gate = jax.nn.sigmoid(dot_split(layer_norm(align), wg_high, wg_low))
        out_ref[s] = align + dot_split(gate * averaged, wo_high, wo_low, dot_t)


def per_device(
    n_row,
    n_col,
    alignment,
    pair_rep,
    seq_mask,
    res_mask,
    left_weight,
    right_weight,
    w_outer,
    w_logits,
    value_weight,
    gate_weight,
    output_weight,
):
    seqs, rows, width = alignment.shape
    cols, pair_width = pair_rep.shape[1], pair_rep.shape[2]
    factor = left_weight.shape[1]
    heads = w_logits.shape[1]
    ratio = cols // rows
    k_col = factor * seqs
    quarter = rows * seqs // 4
    half = n_row // 2
    vmem = pl.BlockSpec(memory_space=pltpu.VMEM)
    smem = pl.BlockSpec(memory_space=pltpu.SMEM)
    dma = pltpu.SemaphoreType.DMA
    left_shape = (quarter + 8, 4 * factor)
    right_shape = (rows + 8, k_col)
    norm_shape = (rows, seqs * width)
    here = 8
    steps = rows // here
    anywhere = pl.BlockSpec(memory_space=pl.ANY)
    full = lambda shape: pl.BlockSpec(shape, lambda i: (0,) * len(shape), pipeline_mode=pl.Buffered(1))
    pair_out, slots, norm_all = pl.pallas_call(
        functools.partial(pair_kernel, n_row, n_col),
        grid=(steps,),
        out_shape=(
            jax.ShapeDtypeStruct(pair_rep.shape, F32),
            jax.ShapeDtypeStruct((n_col, rows * heads, cols), F32),
            jax.ShapeDtypeStruct((n_row,) + norm_shape, F32),
        ),
        in_specs=[
            smem,
            vmem,
            vmem,
            vmem,
            vmem,
            full(w_outer.shape),
            full((heads, pair_width)),
            pl.BlockSpec((here, cols, pair_width), lambda i: (i, 0, 0)),
        ],
        out_specs=(
            pl.BlockSpec((here, cols, pair_width), lambda i: (i, 0, 0)),
            anywhere,
            anywhere,
        ),
        scratch_shapes=[
            pltpu.VMEM((3 * factor, factor * pair_width), BF16),
            pltpu.VMEM((n_col, rows * seqs, 3 * factor), BF16),
            pltpu.VMEM((2 * cols, n_col * k_col), BF16),
            pltpu.VMEM((8, cols), F32),
            pltpu.VMEM((here, n_col, factor // 2, 2 * seqs, pair_width), BF16),
            pltpu.VMEM((here, n_col, factor // 2, 2 * seqs, pair_width), BF16),
            pltpu.VMEM((rows * heads, cols), F32),
            dma((n_col, steps)),
            dma((n_col, steps)),
            dma((steps,)),
            dma((half,)),
            dma((half,)),
            dma((half,)),
            dma((half,)),
            dma,
            pltpu.VMEM((n_col,) + left_shape, F32),
            pltpu.VMEM((n_row,) + right_shape, F32),
            pltpu.VMEM(norm_shape, F32),
            pltpu.VMEM((rows * seqs, width), F32),
            pltpu.VMEM(norm_shape, F32),
            pltpu.VMEM((k_col, seqs * width), F32),
            pltpu.VMEM(left_shape, F32),
            pltpu.VMEM(right_shape, F32),
            dma((n_col,)),
            dma((n_col,)),
            dma((2,)),
            dma((half,)),
            dma((half,)),
            dma((half,)),
            dma((half,)),
        ],
        compiler_params=pltpu.CompilerParams(
            collective_id=0, has_side_effects=True, vmem_limit_bytes=VMEM_LIMIT
        ),
        name="pair",
    )(
        seq_mask,
        res_mask.reshape(1, rows),
        alignment,
        left_weight.T,
        right_weight.T,
        w_outer,
        w_logits.T,
        pair_rep,
    )
    alignment_out = pl.pallas_call(
        average_kernel,
        out_shape=jax.ShapeDtypeStruct(alignment.shape, F32),
        in_specs=[vmem] * 6,
        out_specs=vmem,
        scratch_shapes=[pltpu.VMEM(slots.shape, F32)],
        compiler_params=pltpu.CompilerParams(vmem_limit_bytes=VMEM_LIMIT),
        name="average",
    )(
        slots,
        norm_all.reshape(n_row * rows, seqs * width),
        alignment,
        value_weight,
        gate_weight,
        output_weight.T,
    )
    return (alignment_out, pair_out)


def solution(mesh):
    in_specs = (P("col", "row", None), P("row", "col", None), P("col"), P("row")) + (P(),) * 7
    out_specs = (P("col", "row", None), P("row", "col", None))
    return jax.shard_map(
        functools.partial(per_device, mesh.shape["row"], mesh.shape["col"]),
        mesh=mesh,
        in_specs=in_specs,
        out_specs=out_specs,
        check_vma=False,
    )
```

```python
import functools

import jax
import jax.numpy as jnp
from jax import lax
from jax.experimental import pallas as pl
from jax.experimental.pallas import tpu as pltpu
from jax.sharding import PartitionSpec as P

MESH = pl.DeviceIdType.MESH
F32 = jnp.float32
BF16 = jnp.bfloat16
epsilon = 1e-05
VMEM_LIMIT = 60 * 1024 * 1024


def layer_norm(values):
    center = jnp.mean(values, axis=-1, keepdims=True)
    centred = values - center
    return centred * lax.rsqrt(jnp.mean(centred * centred, axis=-1, keepdims=True) + epsilon)


def split(values):
    high = values.astype(BF16)
    return high, (values - high.astype(F32)).astype(BF16)


def dot(left, right):
    return jnp.dot(left, right, preferred_element_type=F32)


def dot_t(left, right):
    return lax.dot_general(left, right, (((1,), (1,)), ((), ())), preferred_element_type=F32)


def dot_split(left, right_high, right_low, multiply=dot):
    high, low = split(left)
    return multiply(high, right_high) + (multiply(low, right_high) + multiply(high, right_low))


def exchange(
    n_row,
    n_col,
    ratio,
    between,
    seq_ref,
    res_ref,
    align_ref,
    left_w_ref,
    right_w_ref,
    left_out,
    right_out,
    norm_buf,
    rows_buf,
    masked_buf,
    block_buf,
    left_buf,
    right_buf,
    left_send,
    left_recv,
    turn_sem,
    right_send,
    right_recv,
    relay_send,
    relay_recv,
):
    row, col = lax.axis_index("row"), lax.axis_index("col")
    n = n_row * n_col
    me = row * n_col + col
    barrier = pltpu.get_barrier_semaphore()

    def greet(step, carry):
        other = lax.rem(me + step, n)
        pl.semaphore_signal(
            barrier,
            inc=1,
            device_id=(other // n_col, lax.rem(other, n_col)),
            device_id_type=MESH,
        )
        return carry

    lax.fori_loop(1, n, greet, 0)
    seqs, rows, width = align_ref.shape
    res_row = res_ref[...].astype(F32)
    diag = lax.broadcasted_iota(jnp.int32, (rows, rows), 0) == lax.broadcasted_iota(
        jnp.int32, (rows, rows), 1
    )
    res_col = jnp.sum(
        jnp.where(diag, jnp.broadcast_to(res_row, (rows, rows)), 0.0), axis=1, keepdims=True
    )
    factor = right_w_ref.shape[0]
    spread = jnp.broadcast_to(right_w_ref[...][:, None, :], (factor, seqs, width))
    row_seq = lax.broadcasted_iota(jnp.int32, (factor, seqs, width), 1)
    seq_sum = 0.0
    for s in range(seqs):
        normed = layer_norm(align_ref[s])
        norm_buf[:, s * width : (s + 1) * width] = normed
        live = seq_ref[s].astype(F32)
        seq_sum = seq_sum + live
        masked = normed * (res_col * live)
        masked_buf[:, s * width : (s + 1) * width] = masked
        rows_buf[pl.ds(s, rows, stride=seqs), :] = masked
        block_buf[:, s * width : (s + 1) * width] = jnp.where(row_seq == s, spread, 0.0).reshape(
            factor * seqs, width
        )
    wl_high, wl_low = split(left_w_ref[...])
    left = dot_split(rows_buf[...], wl_high, wl_low, dot_t)
    quarter = left.shape[0] // 4
    for g in range(4):
        left_buf[0:quarter, g * factor : (g + 1) * factor] = left[g * quarter : (g + 1) * quarter]
    left_buf[quarter : quarter + 8, :] = jnp.full((8, left_buf.shape[1]), seq_sum, F32)
    wr_high, wr_low = split(block_buf[...])
    right_buf[0:rows, :] = dot_split(masked_buf[...], wr_high, wr_low, dot_t)
    right_buf[rows : rows + 8, 0:rows] = jnp.broadcast_to(res_row, (8, rows))
    right_buf[rows : rows + 8, rows:] = jnp.zeros((8, right_buf.shape[1] - rows), F32)

    pl.semaphore_wait(barrier, n - 1)
    dest = row // ratio
    spot = col * ratio + lax.rem(row, ratio)
    away = dest != col
    half = n_row // 2
    chip, core = row // 2, lax.rem(row, 2)
    partner = 2 * chip + 1 - core

    def peer_row(k):
        return 2 * lax.rem(chip + k, half) + core

    turn = pltpu.make_async_remote_copy(
        right_buf,
        right_out.at[spot],
        turn_sem.at[0],
        turn_sem.at[1],
        device_id=(spot, dest),
        device_id_type=MESH,
    )
    stay = pltpu.make_async_copy(right_buf, right_out.at[spot], turn_sem.at[1])

    @pl.when(away)
    def _():
        turn.start()

    @pl.when(jnp.logical_not(away))
    def _():
        stay.start()

    started = []
    for k in range(1, n_col):
        copy = pltpu.make_async_remote_copy(
            left_buf,
            left_out.at[col],
            left_send.at[k],
            left_recv.at[n_col - k],
            device_id=(row, lax.rem(col + k, n_col)),
            device_id_type=MESH,
        )
        copy.start()
        started.append(copy)
    left_own = pltpu.make_async_copy(left_buf, left_out.at[col], left_recv.at[0])
    left_own.start()
    between()
    pltpu.make_async_copy(right_buf, right_out.at[row], turn_sem.at[1]).wait()
    for k in range(1, half):
        copy = pltpu.make_async_remote_copy(
            right_out.at[row],
            right_out.at[row],
            right_send.at[k],
            right_recv.at[half - k],
            device_id=(peer_row(k), col),
            device_id_type=MESH,
        )
        copy.start()
        started.append(copy)
    for k in range(half):
        src = peer_row(k)
        if k > 0:
            pltpu.make_async_copy(right_buf, right_out.at[src], right_recv.at[k]).wait()
        copy = pltpu.make_async_remote_copy(
            right_out.at[src],
            right_out.at[src],
            relay_send.at[k],
            relay_recv.at[k],
            device_id=(partner, col),
            device_id_type=MESH,
        )
        copy.start()
        started.append(copy)
    left_own.wait()
    for k in range(1, n_col):
        src = lax.rem(col + k, n_col)
        pltpu.make_async_copy(left_buf, left_out.at[src], left_recv.at[k]).wait()
    for k in range(half):
        src = 2 * lax.rem(chip + k, half) + 1 - core
        pltpu.make_async_copy(right_buf, right_out.at[src], relay_recv.at[k]).wait()
    for copy in started:
        copy.wait_send()

    @pl.when(away)
    def _():
        turn.wait_send()


def pair_kernel(
    n_row,
    n_col,
    seq_ref,
    res_ref,
    align_ref,
    left_w_ref,
    right_w_ref,
    outer_ref,
    logits_w_ref,
    pair_ref,
    pair_out,
    slots,
    norm_out,
    w_buf,
    l_buf,
    r_buf,
    mask_buf,
    high_buf,
    low_buf,
    logits_buf,
    logits_send,
    logits_recv,
    logits_own,
    norm_send,
    norm_recv,
    relay_send,
    relay_recv,
    norm_local,
    left_ref,
    right_ref,
    norm_ref,
    *exchange_scratch,
):
    row, col = lax.axis_index("row"), lax.axis_index("col")
    half = n_row // 2
    chip, core = row // 2, lax.rem(row, 2)
    partner = 2 * chip + 1 - core
    quarter = left_ref.shape[1] - 8
    ratio, rows = n_row // n_col, right_ref.shape[1] - 8
    k_col = right_ref.shape[2]
    factor = w_buf.shape[0] // 3
    here, cols, width = pair_ref.shape
    heads = logits_w_ref.shape[0]
    seqs = k_col // factor
    step = pl.program_id(0)
    steps = pl.num_programs(0)

    def peer_row(k):
        return 2 * lax.rem(chip + k, half) + core

    def norm_copy(k):
        return pltpu.make_async_remote_copy(
            norm_ref,
            norm_out.at[row],
            norm_send.at[k],
            norm_recv.at[half - k],
            device_id=(peer_row(k), col),
            device_id_type=MESH,
        )

    def relay_copy(k):
        return pltpu.make_async_remote_copy(
            norm_ref if k == 0 else norm_out.at[peer_row(k)],
            norm_out.at[peer_row(k)],
            relay_send.at[k],
            relay_recv.at[k],
            device_id=(partner, col),
            device_id_type=MESH,
        )

    own_norm = pltpu.make_async_copy(norm_ref, norm_out.at[row], norm_local)
    size = pair_ref.shape[0] * heads

    def logits_copy(k, at):
        part = pl.ds(pl.multiple_of(at * size, size), size)
        return pltpu.make_async_remote_copy(
            logits_buf.at[part],
            slots.at[col, part],
            logits_send.at[k, at],
            logits_recv.at[n_col - k, at],
            device_id=(row, lax.rem(col + k, n_col)),
            device_id_type=MESH,
        )

    def own_logits(at):
        part = pl.ds(pl.multiple_of(at * size, size), size)
        return pltpu.make_async_copy(logits_buf.at[part], slots.at[col, part], logits_own.at[at])

    @pl.when(step == 0)
    def _():
        def between():
            for b in range(factor):
                high, low = split(outer_ref[pl.ds(b, factor, stride=factor), :])
                lanes = slice(b * width, (b + 1) * width)
                w_buf[0:factor, lanes] = high
                w_buf[factor : 2 * factor, lanes] = low
                w_buf[2 * factor : 3 * factor, lanes] = high

        exchange(
            n_row,
            n_col,
            ratio,
            between,
            seq_ref,
            res_ref,
            align_ref,
            left_w_ref,
            right_w_ref,
            left_ref,
            right_ref,
            norm_ref,
            *exchange_scratch,
        )
        own_norm.start()
        count = left_ref[0, quarter : quarter + 1, 0:1]
        for c in range(1, n_col):
            count = count + left_ref[c, quarter : quarter + 1, 0:1]
        scale = 1.0 / jnp.maximum(count, 1.0)
        for c in range(n_col):
            packed = left_ref[c, 0:quarter, :] * scale
            high = packed.astype(BF16).astype(F32)
            low = packed - high
            for g in range(4):
                lanes = slice(g * factor, (g + 1) * factor)
                parts = [high[:, lanes], high[:, lanes], low[:, lanes]]
                l_buf[c, g * quarter : (g + 1) * quarter, :] = jnp.concatenate(
                    parts, axis=1
                ).astype(BF16)
            for t in range(ratio):
                high_r, low_r = split(right_ref[c * ratio + t, 0:rows, :])
                lanes = slice(c * k_col, (c + 1) * k_col)
                r_buf[t * rows : (t + 1) * rows, lanes] = high_r
                r_buf[cols + t * rows : cols + (t + 1) * rows, lanes] = low_r
        for t in range(ratio):
            mask_buf[:, t * rows : (t + 1) * rows] = (
                right_ref[t, rows : rows + 8, 0:rows] - 1.0
            ) * 1000000000.0

    group = here * seqs
    l_rows = jnp.concatenate(
        [l_buf[c, pl.ds(pl.multiple_of(step * group, group), group), :] for c in range(n_col)],
        axis=0,
    )
    for nb in range(factor // 2):
        mixed = dot(l_rows, w_buf[:, nb * 2 * width : (nb + 1) * 2 * width])
        tiles = jnp.concatenate(
            [
                mixed[:, :width].reshape(n_col * here, seqs, width),
                mixed[:, width:].reshape(n_col * here, seqs, width),
            ],
            axis=1,
        )
        high, low = split(tiles)
        for c in range(n_col):
            high_buf[:, c, nb] = high[c * here : (c + 1) * here]
            low_buf[:, c, nb] = low[c * here : (c + 1) * here]
    depth = n_col * k_col
    r_both = r_buf[...]
    w_high, w_low = split(logits_w_ref[...])
    w_both = jnp.concatenate([w_high.astype(F32), w_low.astype(F32)], axis=0).astype(BF16)
    for p in range(here // 2):
        right_high = jnp.concatenate(
            [high_buf[2 * p + t].reshape(depth, width) for t in range(2)], axis=1
        )
        right_low = jnp.concatenate(
            [low_buf[2 * p + t].reshape(depth, width) for t in range(2)], axis=1
        )
        first = dot(r_both, right_high)
        sums = first[:cols] + (first[cols:] + dot(r_both[:cols], right_low))
        for t in range(2):
            i = 2 * p + t
            pair_out[i] = pair_ref[i] + sums[:, t * width : (t + 1) * width]
    batch = here // 2
    for g in range(0, here, batch):
        pairs = pair_out[g : g + batch].reshape(batch * cols, width)
        high, low = split(layer_norm(pairs))
        for t in range(batch):
            one = dot_t(w_both, high[t * cols : (t + 1) * cols])
            two = dot_t(w_both, low[t * cols : (t + 1) * cols])
            logits = one[:heads] + (one[heads:] + two[:heads])
            start = pl.multiple_of(step * size + (g + t) * heads, heads)
            logits_buf[pl.ds(start, heads), :] = logits + mask_buf[...]

    @pl.when(step == 0)
    def _():
        relay_copy(0).start()
        for k in range(1, half):
            norm_copy(k).start()

    for k in range(1, n_col):
        logits_copy(k, step).start()
    own_logits(step).start()

    @pl.when(step == steps // 2)
    def _():
        for k in range(1, half):
            pltpu.make_async_copy(norm_ref, norm_out.at[peer_row(k)], norm_recv.at[k]).wait()
            relay_copy(k).start()

    @pl.when(step == steps - 1)
    def _():
        own_norm.wait()
        for k in range(half):
            other = 2 * lax.rem(chip + k, half) + 1 - core
            relay_copy(k).wait_send()
            pltpu.make_async_copy(norm_ref, norm_out.at[other], relay_recv.at[k]).wait()
        for k in range(1, half):
            norm_copy(k).wait_send()

        def drain(at, carry):
            own_logits(at).wait()
            part = pl.ds(pl.multiple_of(at * size, size), size)
            for k in range(1, n_col):
                logits_copy(k, at).wait_send()
                src = lax.rem(col + k, n_col)
                pltpu.make_async_copy(
                    logits_buf.at[part], slots.at[src, part], logits_recv.at[k, at]
                ).wait()
            return carry

        lax.fori_loop(0, steps, drain, 0)


def average_kernel(
    slots,
    norm_ref,
    align_ref,
    value_w_ref,
    gate_w_ref,
    output_w_ref,
    pair_ref,
    out_ref,
    pair_out,
    terms_buf,
    pair_buf,
    pair_sem,
):
    bring = pltpu.make_async_copy(pair_ref, pair_buf, pair_sem.at[0])
    bring.start()
    seqs, rows, width = align_ref.shape
    n_col, total_rows, cols = slots.shape
    heads = total_rows // rows
    channels = value_w_ref.shape[1]
    head_width = channels // heads
    wv_high, wv_low = split(value_w_ref[...])
    wg_high, wg_low = split(gate_w_ref[...])
    wo_high, wo_low = split(output_w_ref[...])
    own_head = (
        lax.broadcasted_iota(jnp.int32, (heads, channels), 1) // head_width
        == lax.broadcasted_iota(jnp.int32, (heads, channels), 0)
    ).astype(F32)
    top = jnp.max(slots[0], axis=1, keepdims=True)
    for c in range(1, n_col):
        top = jnp.maximum(top, jnp.max(slots[c], axis=1, keepdims=True))
    total = jnp.zeros_like(top)
    for c in range(n_col):
        terms = jnp.exp(slots[c] - top)
        terms_buf[c] = terms
        total = total + jnp.sum(terms, axis=1, keepdims=True)
    inverse = 1.0 / total
    mixed = None
    for c in range(n_col):
        high, low = split(norm_ref[c * cols : (c + 1) * cols, :])
        part = dot_split(terms_buf[c] * inverse, high, low)
        mixed = part if mixed is None else mixed + part
    bring.wait()
    place = pltpu.make_async_copy(pair_buf, pair_out, pair_sem.at[1])
    place.start()
    for s in range(seqs):
        wide = dot_split(mixed[:, s * width : (s + 1) * width], wv_high, wv_low)
        averaged = jnp.sum(wide.reshape(rows, heads, channels) * own_head[None], axis=1)
        align = align_ref[s]
        gate = jax.nn.sigmoid(dot_split(layer_norm(align), wg_high, wg_low))
        out_ref[s] = align + dot_split(gate * averaged, wo_high, wo_low, dot_t)
    place.wait()


def per_device(
    n_row,
    n_col,
    alignment,
    pair_rep,
    seq_mask,
    res_mask,
    left_weight,
    right_weight,
    w_outer,
    w_logits,
    value_weight,
    gate_weight,
    output_weight,
):
    seqs, rows, width = alignment.shape
    cols, pair_width = pair_rep.shape[1], pair_rep.shape[2]
    factor = left_weight.shape[1]
    heads = w_logits.shape[1]
    ratio = cols // rows
    k_col = factor * seqs
    quarter = rows * seqs // 4
    half = n_row // 2
    vmem = pl.BlockSpec(memory_space=pltpu.VMEM)
    smem = pl.BlockSpec(memory_space=pltpu.SMEM)
    dma = pltpu.SemaphoreType.DMA
    left_shape = (quarter + 8, 4 * factor)
    right_shape = (rows + 8, k_col)
    norm_shape = (rows, seqs * width)
    here = 8
    steps = rows // here
    anywhere = pl.BlockSpec(memory_space=pl.ANY)
    full = lambda shape: pl.BlockSpec(shape, lambda i: (0,) * len(shape), pipeline_mode=pl.Buffered(1))
    pair_out, slots, norm_all = pl.pallas_call(
        functools.partial(pair_kernel, n_row, n_col),
        grid=(steps,),
        out_shape=(
            jax.ShapeDtypeStruct(pair_rep.shape, F32),
            jax.ShapeDtypeStruct((n_col, rows * heads, cols), F32),
            jax.ShapeDtypeStruct((n_row,) + norm_shape, F32),
        ),
        in_specs=[
            smem,
            vmem,
            vmem,
            vmem,
            vmem,
            full(w_outer.shape),
            full((heads, pair_width)),
            pl.BlockSpec((here, cols, pair_width), lambda i: (i, 0, 0)),
        ],
        out_specs=(
            pl.BlockSpec((here, cols, pair_width), lambda i: (i, 0, 0)),
            anywhere,
            anywhere,
        ),
        scratch_shapes=[
            pltpu.VMEM((3 * factor, factor * pair_width), BF16),
            pltpu.VMEM((n_col, rows * seqs, 3 * factor), BF16),
            pltpu.VMEM((2 * cols, n_col * k_col), BF16),
            pltpu.VMEM((8, cols), F32),
            pltpu.VMEM((here, n_col, factor // 2, 2 * seqs, pair_width), BF16),
            pltpu.VMEM((here, n_col, factor // 2, 2 * seqs, pair_width), BF16),
            pltpu.VMEM((rows * heads, cols), F32),
            dma((n_col, steps)),
            dma((n_col, steps)),
            dma((steps,)),
            dma((half,)),
            dma((half,)),
            dma((half,)),
            dma((half,)),
            dma,
            pltpu.VMEM((n_col,) + left_shape, F32),
            pltpu.VMEM((n_row,) + right_shape, F32),
            pltpu.VMEM(norm_shape, F32),
            pltpu.VMEM((rows * seqs, width), F32),
            pltpu.VMEM(norm_shape, F32),
            pltpu.VMEM((k_col, seqs * width), F32),
            pltpu.VMEM(left_shape, F32),
            pltpu.VMEM(right_shape, F32),
            dma((n_col,)),
            dma((n_col,)),
            dma((2,)),
            dma((half,)),
            dma((half,)),
            dma((half,)),
            dma((half,)),
        ],
        compiler_params=pltpu.CompilerParams(
            collective_id=0, has_side_effects=True, vmem_limit_bytes=VMEM_LIMIT
        ),
        name="pair",
    )(
        seq_mask,
        res_mask.reshape(1, rows),
        alignment,
        left_weight.T,
        right_weight.T,
        w_outer,
        w_logits.T,
        pair_rep,
    )
    alignment_out, pair_final = pl.pallas_call(
        average_kernel,
        out_shape=(
            jax.ShapeDtypeStruct(alignment.shape, F32),
            jax.ShapeDtypeStruct(pair_rep.shape, F32),
        ),
        in_specs=[vmem] * 6 + [anywhere],
        out_specs=(vmem, anywhere),
        scratch_shapes=[
            pltpu.VMEM(slots.shape, F32),
            pltpu.VMEM(pair_rep.shape, F32),
            dma((2,)),
        ],
        compiler_params=pltpu.CompilerParams(vmem_limit_bytes=VMEM_LIMIT),
        name="average",
    )(
        slots,
        norm_all.reshape(n_row * rows, seqs * width),
        alignment,
        value_weight,
        gate_weight,
        output_weight.T,
        pair_out,
    )
    return (alignment_out, pair_final)


def solution(mesh):
    in_specs = (P("col", "row", None), P("row", "col", None), P("col"), P("row")) + (P(),) * 7
    out_specs = (P("col", "row", None), P("row", "col", None))
    return jax.shard_map(
        functools.partial(per_device, mesh.shape["row"], mesh.shape["col"]),
        mesh=mesh,
        in_specs=in_specs,
        out_specs=out_specs,
        check_vma=False,
    )
```
